512 devices in a mesh: section: 8 (over z_hi, x), expert: 64 (over y, z_lo, core).
Axes of the slice: x: 4, y: 4, z: 16 (z_hi: 2, z_lo: 8; z = z_hi * 8 + z_lo), core: 2. Of those that a mesh axis runs over, the one named last changes fastest.
Arguments:
- hidden: bfloat16 [8, 512, 7168], P('section', 'expert'), may hold values from -6 to 6
- norm_gain: float32 [8, 7168], P('section'), may hold values from 0.25 to 1.75
- w_up: bfloat16 [8, 7168, 8192], P('section', None, 'expert'), may hold values from -0.0625 to 0.0625
- w_down: bfloat16 [8, 8192, 7168], P('section', 'expert'), may hold values from -0.1875 to 0.1875
- expert_ids: int32 [8, 2, 512, 2], P('section', None, 'expert'), may hold values from 0 to 7, all different within a row; in each aligned block of 8 rows (0 to 7, 8 to 15, ..., all dimensions but the last counted through in order) at most 4 rows name the same one
- route_gates: float32 [8, 2, 512, 2], P('section', None, 'expert'), may hold values from 0.25 to 1.5
Outputs:
- advanced: bfloat16 [8, 512, 7168], P('section', 'expert')
The draws below stay inside these ranges and needn't reach their ends.
Inputs may be any that keep to these rules, and one draw needn't show every extreme that they name: `expert_ids`: the 2 ids of a row differ. In each aligned block of 8 rows (the rows of one device in one pass) no expert is named by more than 4 rows; some expert is named by exactly 4 rows.
All inputs are finite; a program needn't handle non-finite values.
Results may differ from the reference program's by a relative error of at most 0.0085.
Values may be sent and summed in bfloat16 or wider, within the bound.
No kernel may reach another device: no remote copies, remote signals or barrier semaphores. Data moves between devices by JAX's collectives and lax.ppermute only.
A program may use at most 64 MiB of HBM per device.

```python
import math
import jax
import jax.numpy as jnp
import numpy as np
from jax import lax

D = 7168
HID = 1024
HID_DEV = 128
TOP = 2
ITERS = 2
ROWS_DEV = 8
GROUP = 8
EXPERTS_SECTION = 8
CAP = 4
MBROWS = 512
SECTIONS = 8
N_EXPERT = 64


def block_levels(rng, extent, shards, least, largest):
    loudness = 1.0
    for dim, blocks in shards:
        steps = jax.random.uniform(jax.random.fold_in(jax.random.fold_in(rng, 6), dim), (blocks,), jnp.float32, least / len(shards), largest / len(shards))
        loudness = loudness * jnp.repeat(jnp.exp(steps), extent[dim] // blocks).reshape((-1,) + (1,) * (len(extent) - 1 - dim))
    return loudness


def routed_block(own_key, own, number, rows, count, top, reach, lean):
    ranking = jax.random.permutation(own_key, count)
    crowded, usual = load_shares(count, rows * top, reach, lean, True), load_shares(count, rows * top, reach, lean, False)
    places = jnp.arange(count)

    def named(lengths, rotation):
        used = int((lengths > 0).sum())
        fixed = max(1, used // 4)
        passed = fixed + (places - fixed + rotation * (used - fixed)) % max(1, count - fixed)
        return jnp.zeros((count,), jnp.int32).at[ranking[jnp.where(places < fixed, places, passed)]].set(jnp.asarray(lengths, jnp.int32))

    lengths = jnp.where(number % 4 == 0, named(crowded, number // 4), named(usual, number - number // 4 - 1))
    mixed = jax.random.permutation(jax.random.fold_in(own, 3), count)
    source_of, receiver = mixed[0:count // 2 * 2:2], mixed[1:count // 2 * 2:2]
    room = jnp.minimum(lengths[source_of] - 1, reach - lengths[receiver]) // 2
    room = jnp.where((source_of == ranking[0]) | (receiver == ranking[0]) | (lengths[receiver] == 0), 0, jnp.maximum(room, 0))
    passed = jax.random.randint(jax.random.fold_in(own, 4), (count // 2,), 0, 1 << 20) % (room + 1)
    lengths = lengths.at[source_of].add(-passed).at[receiver].add(passed)
    items = jnp.searchsorted(jnp.cumsum(lengths), jnp.arange(rows * top), side="right").astype(jnp.int32)
    grid = items.reshape(top, rows).T
    grid = grid[jax.random.permutation(jax.random.fold_in(own, 1), rows)]
    rotation = jax.random.randint(jax.random.fold_in(own, 2), (rows, 1), 0, top)
    return jnp.take_along_axis(grid, (jnp.arange(top)[None, :] + rotation) % top, axis=1)


def load_shares(amount, total, reach, skew, full):
    portions = [(1 << 20) // math.isqrt(rank ** skew) + 1 for rank in range(1, amount + 1)]
    largest = reach if full else min(reach, max(-(-total // amount), total * portions[0] // sum(portions)))
    least = 1 if total - largest >= amount - 1 else 0
    counts, surplus = [largest] + [least] * (amount - 1), total - largest - least * (amount - 1)
    while surplus > 0:
        candidates = [i for i in range(1, amount) if counts[i] < largest] or [i for i in range(1, amount) if counts[i] < reach]
        mass, budget = sum([portions[i] for i in candidates]), surplus
        for i in candidates:
            addition = min(reach - counts[i], max(1, budget * portions[i] // mass), surplus)
            counts[i] = counts[i] + addition
            surplus = surplus - addition
    return np.array(counts)


def bell_draw(key, extent, width, reach, cuts=(), held_as=jnp.bfloat16):
    result = jax.random.normal(key, extent, jnp.float32) * width
    if len(cuts) > 0:
        result = block_levels(key, extent, cuts, -0.22, 0.18) * result
    return jnp.clip(result, min=-reach, max=reach).astype(held_as)


def setup_inputs(seed: int = 0) -> dict:
    seeds = jax.random.split(jax.random.key(seed), 7)
    hidden = bell_draw(seeds[0], (SECTIONS, MBROWS, D), 1.0, 6.0, ((0, 8), (1, 64)))
    norm_gain = jnp.clip(1.0 + 0.15 * jax.random.normal(seeds[1], (SECTIONS, D), jnp.float32), 0.25, 1.75)
    w_up = bell_draw(seeds[2], (SECTIONS, D, EXPERTS_SECTION * HID), D ** -0.5, 0.0625, ((0, 8), (2, 64)))
    w_down = bell_draw(seeds[3], (SECTIONS, EXPERTS_SECTION * HID, D), HID ** -0.5, 0.1875, ((0, 8), (1, 64)))
    expert_ids_keys = jax.random.split(jax.random.fold_in(seeds[4], 1), SECTIONS * ITERS * MBROWS // ROWS_DEV)
    expert_ids_turns = jax.random.permutation(jax.random.fold_in(seeds[4], 3), SECTIONS * ITERS * MBROWS // ROWS_DEV)
    expert_ids = jax.vmap(lambda own, number: routed_block(jax.random.fold_in(seeds[4], 2), own, number, ROWS_DEV, EXPERTS_SECTION, TOP, CAP, 2))(expert_ids_keys, expert_ids_turns).reshape((SECTIONS, ITERS, MBROWS, TOP))
    route_gates = jnp.clip(0.25 + 1.25 * jax.random.uniform(seeds[5], (SECTIONS, ITERS, MBROWS, TOP), jnp.float32) ** block_levels(seeds[5], (SECTIONS, ITERS, MBROWS, TOP), ((0, 8), (2, 64)), -0.2, 0.2), 0.25, 1.5)
    return {"hidden": hidden, "norm_gain": norm_gain, "w_up": w_up, "w_down": w_down, "expert_ids": expert_ids, "route_gates": route_gates}


def layer(operands):
    current, gain_row, up_weight, down_weight, route_ids, gate_values = operands
    values = current.astype(jnp.float32)
    inverse_rms = lax.rsqrt(lax.optimization_barrier(jnp.mean(values * values, axis=-1, keepdims=True)) + 1e-06)
    normed = (values * inverse_rms * gain_row.astype(jnp.float32)).astype(jnp.bfloat16)
    row_count = current.shape[0]
    top_count = route_ids.shape[1]
    slot_count = N_EXPERT * CAP
    flat_ids = route_ids.reshape(-1).astype(jnp.int32)
    onehot = (flat_ids[:, None] == jnp.arange(EXPERTS_SECTION, dtype=jnp.int32)[None, :]).astype(jnp.int32)
    earlier = jnp.cumsum(onehot, axis=0) - onehot
    slot_index = lax.optimization_barrier(jnp.sum(earlier * onehot, axis=1)).astype(jnp.int32)
    target = (flat_ids * slot_count + slot_index).astype(jnp.int32)
    source_rows = (jnp.arange(row_count * top_count, dtype=jnp.int32) // top_count).astype(jnp.int32)
    holder = jnp.zeros((EXPERTS_SECTION * slot_count,), jnp.int32).at[target].set(source_rows)
    filled = jnp.zeros((EXPERTS_SECTION * slot_count,), jnp.float32).at[target].set(1.0)
    gathered = normed[holder] * filled[:, None].astype(jnp.bfloat16)
    batches = gathered.reshape(EXPERTS_SECTION, slot_count, D)

    def one_expert(inputs):
        rows_in, expert_index = inputs
        up_part = lax.dynamic_slice_in_dim(up_weight, (expert_index * HID).astype(jnp.int32), HID, 1)
        down_part = lax.dynamic_slice_in_dim(down_weight, (expert_index * HID).astype(jnp.int32), HID, 0)
        upward = jnp.dot(rows_in, up_part, preferred_element_type=jnp.float32)
        active = jax.nn.silu(upward).astype(jnp.bfloat16)
        pieces = jnp.einsum('sgh,ghd->sgd', active.reshape(slot_count, GROUP, HID_DEV).astype(jnp.float32), down_part.reshape(GROUP, HID_DEV, D).astype(jnp.float32), precision=lax.Precision.HIGHEST)
        rounded = lax.optimization_barrier(pieces.astype(jnp.bfloat16))
        return lax.optimization_barrier(jnp.sum(rounded.astype(jnp.float32), axis=1))
    outputs = lax.map(one_expert, (batches, jnp.arange(EXPERTS_SECTION, dtype=jnp.int32)))
    chosen = outputs.reshape(-1, D)[target]
    weighted = chosen * gate_values.reshape(-1)[:, None].astype(jnp.float32)
    mixture = lax.optimization_barrier(jnp.sum(weighted.reshape(row_count, top_count, D), axis=1))
    return (values + mixture).astype(jnp.bfloat16)

def reference(hidden, norm_gain, w_up, w_down, expert_ids, route_gates):
    current = hidden
    for pass_index in range(ITERS):
        advanced = lax.map(layer, (current, norm_gain, w_up, w_down, expert_ids[:, pass_index], route_gates[:, pass_index]))
        current = jnp.roll(advanced, 1, axis=0)
    return current
```

```python
import jax
import jax.numpy as jnp
from jax import lax
from jax.sharding import PartitionSpec as P

HID = 1024
HID_DEV = 128


def shifted(value, axis, by):
    count = lax.axis_size(axis)
    return lax.ppermute(value, axis, [(i, (i + by) % count) for i in range(count)])


def rms_scale(current, gain_row):
    values = current.astype(jnp.float32)
    inverse_rms = lax.rsqrt(jnp.mean(values * values, axis=-1, keepdims=True) + 1e-06)
    return (values, (values * inverse_rms * gain_row).astype(jnp.bfloat16))


def route_tables(route_ids, gate_values, expert_count, capacity):
    row_count, top_count = route_ids.shape
    flat_ids = route_ids.reshape(-1)
    order = jnp.arange(row_count * top_count, dtype=jnp.int32)
    same = (flat_ids[:, None] == flat_ids[None, :]) & (order[None, :] < order[:, None])
    slot_index = jnp.sum(same.astype(jnp.int32), axis=1)
    target = flat_ids * capacity + slot_index
    placed = (
        jnp.arange(expert_count * capacity, dtype=jnp.int32)[:, None] == target[None, :]
    ).astype(jnp.float32)
    owners = (
        (jnp.arange(row_count * top_count, dtype=jnp.int32) // top_count)[:, None]
        == jnp.arange(row_count, dtype=jnp.int32)[None, :]
    ).astype(jnp.float32)
    picker = jnp.dot(placed, owners, precision=lax.Precision.HIGHEST)
    weigher = jnp.dot(
        placed * gate_values.reshape(-1)[None, :], owners, precision=lax.Precision.HIGHEST
    )
    return (picker.astype(jnp.bfloat16), weigher)


def expert_apply(received, up_slice, down_slice):
    flat_rows = received.reshape(-1, received.shape[-1])
    upward = jnp.dot(flat_rows, up_slice, preferred_element_type=jnp.float32)
    active = jax.nn.silu(upward).astype(jnp.bfloat16)
    partial_out = jnp.dot(active, down_slice, preferred_element_type=jnp.float32).astype(
        jnp.bfloat16
    )
    return partial_out.reshape(received.shape)


def body(hidden, norm_gain, w_up, w_down, expert_ids, route_gates):
    model_width = hidden.shape[-1]
    group_size = HID // HID_DEV
    devices = lax.axis_size("expert")
    expert_count = devices // group_size
    row_count = hidden.shape[1]
    top_count = expert_ids.shape[-1]
    capacity = min(row_count, (row_count * top_count + expert_count - 1) // expert_count + 2)
    up_slice = w_up[0]
    down_slice = w_down[0]
    gain_row = norm_gain[0]
    current = hidden[0]
    for pass_index in range(expert_ids.shape[1]):
        values, normed = rms_scale(current, gain_row)
        picker, weigher = route_tables(
            expert_ids[0, pass_index], route_gates[0, pass_index], expert_count, capacity
        )
        packed = jnp.dot(picker, normed, preferred_element_type=jnp.float32).astype(jnp.bfloat16)
        copies = jnp.broadcast_to(
            packed.reshape(expert_count, 1, capacity, model_width),
            (expert_count, group_size, capacity, model_width),
        )
        copies = copies.reshape(devices, capacity, model_width)
        partial_out = expert_apply(
            lax.all_to_all(copies, "expert", split_axis=0, concat_axis=0, tiled=True),
            up_slice,
            down_slice,
        )
        returned = lax.all_to_all(partial_out, "expert", split_axis=0, concat_axis=0, tiled=True)
        outputs = jnp.sum(
            returned.reshape(expert_count, group_size, capacity, model_width).astype(jnp.float32),
            axis=1,
        )
        mixture = jnp.dot(
            weigher.T,
            outputs.reshape(expert_count * capacity, model_width),
            precision=lax.Precision.HIGHEST,
            preferred_element_type=jnp.float32,
        )
        updated = (values + mixture).astype(jnp.bfloat16)
        current = shifted(updated, "section", 1)
    return current[None]


def solution(mesh):
    placed = (
        P("section", "expert", None),
        P("section", None),
        P("section", None, "expert"),
        P("section", "expert", None),
        P("section", None, "expert", None),
        P("section", None, "expert", None),
    )
    return jax.shard_map(
        body, mesh=mesh, in_specs=placed, out_specs=P("section", "expert", None), check_vma=False
    )
```

```python
import jax
import jax.numpy as jnp
from jax import lax
from jax.sharding import PartitionSpec as P

HID = 1024
HID_DEV = 128
GROUP = HID // HID_DEV
CAP = 4
HALVES = 2
LANES = 128


def groups(count):
    span = GROUP * HALVES
    same_expert = [[first + j for j in range(GROUP)] for first in range(0, count, GROUP)]
    same_row = [[first + k for k in range(span)] for first in range(0, count, span)]
    same_slice = [[first + k for first in range(0, count, span)] for k in range(span)]
    return same_expert, same_row, same_slice


def exchange(value, within):
    return lax.all_to_all(
        value, "expert", split_axis=0, concat_axis=0, axis_index_groups=within, tiled=True
    )


def other_half(value):
    count = lax.axis_size("expert")
    return lax.ppermute(value, "expert", [(i, i ^ GROUP) for i in range(count)])


def next_section(value):
    count = lax.axis_size("section")
    return lax.ppermute(value, "section", [(i, (i + 1) % count) for i in range(count)])


def head(value):
    return lax.reduce_precision(value, exponent_bits=8, mantissa_bits=7)


def in_three(value):
    first = head(value)
    second = head(value - first)
    third = head(value - first - second)
    return [part.astype(jnp.bfloat16) for part in (first, second, third)]


def tables(ids, gates, half, peers, rows_dev):
    rows = ids.shape[0]
    wanted = 2 * jnp.arange(peers, dtype=jnp.int32) + half
    hit = ids.T[None, :, :] == wanted[:, None, None]
    routed = jnp.any(hit, axis=1)
    weight = jnp.sum(jnp.where(hit, gates.T[None, :, :], 0.0), axis=1)
    at = jnp.arange(rows, dtype=jnp.int32)
    before = (at[:, None] < at[None, :]) & (at[:, None] // rows_dev == at[None, :] // rows_dev)
    rank = jnp.dot(
        routed.astype(jnp.bfloat16), before.astype(jnp.bfloat16), preferred_element_type=jnp.float32
    ).astype(jnp.int32)
    slots = rows // rows_dev * CAP
    slot = jnp.arange(slots, dtype=jnp.int32)
    mine = (slot[:, None] // CAP == at[None, :] // rows_dev)[None]
    picked = mine & routed[:, None, :] & (rank[:, None, :] == (slot % CAP)[None, :, None])
    weigher = jnp.where(picked, weight[:, None, :], 0.0)
    shape = (peers * slots, rows)
    return picked.astype(jnp.bfloat16).reshape(shape), weigher.reshape(shape)


def body(hidden, norm_gain, w_up, w_down, expert_ids, route_gates):
    width = hidden.shape[-1]
    rows_dev = hidden.shape[1]
    passes, top = expert_ids.shape[1], expert_ids.shape[-1]
    count = lax.axis_size("expert")
    peers = count // (GROUP * HALVES)
    part = width // GROUP
    block = GROUP * rows_dev
    same_expert, same_row, same_slice = groups(count)
    place = lax.axis_index("expert")
    half = place // GROUP % HALVES

    facts = [expert_ids[0].astype(jnp.bfloat16)] + in_three(route_gates[0])
    facts = jnp.stack(facts).transpose(2, 0, 1, 3).reshape(rows_dev, -1)
    facts = jnp.pad(facts, ((0, 0), (0, LANES - facts.shape[1])))
    sliced = hidden[0].reshape(rows_dev, GROUP, part).transpose(1, 0, 2)
    sliced = jnp.concatenate(
        [sliced, jnp.broadcast_to(facts[None], (GROUP, rows_dev, LANES))], axis=2
    )
    arrived = exchange(jnp.concatenate([sliced, sliced]), same_row)
    arrived = arrived.reshape(HALVES, block, part + LANES)
    arrived = lax.dynamic_slice_in_dim(jnp.concatenate([arrived, arrived]), half, HALVES, 0)
    arrived = arrived.reshape(HALVES * block, part + LANES)
    rows = arrived[:, :part]
    facts = arrived[:, part:].astype(jnp.float32)
    routes = facts[:, : 4 * passes * top].reshape(HALVES * block, 4, passes, top)

    up = exchange(w_up[0].reshape(GROUP, part, HID_DEV), same_expert)
    up = up.transpose(1, 0, 2).reshape(part, HID)
    down = exchange(w_down[0].reshape(HID_DEV, GROUP, part).transpose(1, 0, 2), same_expert)
    down = down.reshape(HID, part)
    gain = lax.dynamic_slice_in_dim(norm_gain[0], place % GROUP * part, part, 0)

    for t in range(passes):
        ids = routes[:, 0, t].astype(jnp.int32)
        gates = jnp.sum(routes[:, 1:, t], axis=1)
        picker, weigher = tables(ids, gates, half, peers, rows_dev)
        slots = jnp.dot(picker, rows, preferred_element_type=jnp.float32).astype(jnp.bfloat16)
        slots = exchange(slots, same_slice)
        values = slots.astype(jnp.float32)
        squares = jnp.sum(values * values, axis=1)
        partial = jnp.dot(
            (values * gain).astype(jnp.bfloat16), up, preferred_element_type=jnp.float32
        ).astype(jnp.bfloat16)
        held = slots.shape[0]
        partial = partial.reshape(held, GROUP, HID_DEV).transpose(1, 0, 2)
        big = head(squares)
        beside = jnp.stack([big, squares - big]).astype(jnp.bfloat16).reshape(-1, LANES)
        beside = jnp.pad(beside, ((0, 16 - beside.shape[0]), (0, 0)))
        beside = jnp.broadcast_to(beside[None], (GROUP, 16, LANES))
        sums = jnp.sum(
            exchange(jnp.concatenate([partial, beside], axis=1), same_expert).astype(jnp.float32),
            axis=0,
        )
        squares = jnp.sum(sums[held:].reshape(-1)[: 2 * held].reshape(2, held), axis=0)
        scale = lax.rsqrt(squares / width + 1e-06)
        active = jax.nn.silu(sums[:held] * scale[:, None]).astype(jnp.bfloat16)
        active = lax.all_gather(active, "expert", axis_index_groups=same_expert)
        active = active.transpose(1, 0, 2).reshape(held, HID)
        outputs = jnp.dot(active, down, preferred_element_type=jnp.float32).astype(jnp.bfloat16)
        outputs = exchange(outputs, same_slice)
        mixture = jnp.dot(
            weigher.T,
            outputs.astype(jnp.float32),
            precision=lax.Precision.HIGHEST,
            preferred_element_type=jnp.float32,
        )
        own = rows[:block].astype(jnp.float32) + mixture[:block]
        other = mixture[block:].astype(jnp.bfloat16)
        if t + 1 < passes:
            own = (own + other_half(other).astype(jnp.float32)).astype(jnp.bfloat16)
            own = next_section(own)
            rows = jnp.concatenate([own, other_half(own)])
        else:
            own = own.astype(jnp.bfloat16)
            both = lax.dynamic_slice_in_dim(jnp.stack([own, other, own]), half, HALVES, 0)
            both = exchange(both.reshape(HALVES * GROUP, rows_dev, part), same_row)
            both = both.reshape(HALVES, GROUP, rows_dev, part).astype(jnp.float32)
            done = jnp.sum(both, axis=0).astype(jnp.bfloat16)
            done = next_section(done.transpose(1, 0, 2).reshape(rows_dev, width))
    return done[None]


def solution(mesh):
    placed = (
        P("section", "expert", None),
        P("section", None),
        P("section", None, "expert"),
        P("section", "expert", None),
        P("section", None, "expert", None),
        P("section", None, "expert", None),
    )
    return jax.shard_map(
        body, mesh=mesh, in_specs=placed, out_specs=P("section", "expert", None), check_vma=False
    )
```

```python
import jax
import jax.numpy as jnp
from jax import lax
from jax.sharding import PartitionSpec as P

HID = 1024
HID_DEV = 128
GROUP = HID // HID_DEV
CAP = 4
HALVES = 2
LANES = 128


def groups(count):
    span = GROUP * HALVES
    same_expert = [[first + j for j in range(GROUP)] for first in range(0, count, GROUP)]
    same_row = [[first + k for k in range(span)] for first in range(0, count, span)]
    same_slice = [[first + k for first in range(0, count, span)] for k in range(span)]
    return same_expert, same_row, same_slice


def exchange(value, within):
    return lax.all_to_all(
        value, "expert", split_axis=0, concat_axis=0, axis_index_groups=within, tiled=True
    )


def other_half(value):
    count = lax.axis_size("expert")
    return lax.ppermute(value, "expert", [(i, i ^ GROUP) for i in range(count)])


def next_section(value):
    sections, count = lax.axis_size("section"), lax.axis_size("expert")
    route = [
        (s * count + i, (s + 1) % sections * count + (i ^ GROUP))
        for s in range(sections)
        for i in range(count)
    ]
    return lax.ppermute(value, ("section", "expert"), route)


def spread(slices, place):
    count = lax.axis_size("expert")
    return [
        lax.ppermute(
            lax.dynamic_index_in_dim(slices, place % GROUP ^ step, 0),
            "expert",
            [(i, i ^ step) for i in range(count)],
        )
        for step in range(1, GROUP)
    ]


def gathered(slices, came, place):
    for step in range(1, GROUP):
        slices = lax.dynamic_update_slice_in_dim(
            slices, came[step - 1], place % GROUP ^ step, 0
        )
    return slices


def head(value):
    return lax.reduce_precision(value, exponent_bits=8, mantissa_bits=7)


def in_three(value):
    first = head(value)
    second = head(value - first)
    third = head(value - first - second)
    return [part.astype(jnp.bfloat16) for part in (first, second, third)]


def tables(ids, gates, half, peers, rows_dev):
    rows = ids.shape[0]
    wanted = 2 * jnp.arange(peers, dtype=jnp.int32) + half
    hit = ids.T[None, :, :] == wanted[:, None, None]
    routed = jnp.any(hit, axis=1)
    weight = jnp.sum(jnp.where(hit, gates.T[None, :, :], 0.0), axis=1)
    at = jnp.arange(rows, dtype=jnp.int32)
    before = (at[:, None] < at[None, :]) & (at[:, None] // rows_dev == at[None, :] // rows_dev)
    rank = jnp.dot(
        routed.astype(jnp.bfloat16), before.astype(jnp.bfloat16), preferred_element_type=jnp.float32
    ).astype(jnp.int32)
    slots = rows // rows_dev * CAP
    slot = jnp.arange(slots, dtype=jnp.int32)
    mine = (slot[:, None] // CAP == at[None, :] // rows_dev)[None]
    picked = mine & routed[:, None, :] & (rank[:, None, :] == (slot % CAP)[None, :, None])
    weigher = jnp.where(picked, weight[:, None, :], 0.0)
    shape = (peers * slots, rows)
    return picked.astype(jnp.bfloat16).reshape(shape), weigher.reshape(shape)


def body(hidden, norm_gain, w_up, w_down, expert_ids, route_gates):
    width = hidden.shape[-1]
    rows_dev = hidden.shape[1]
    passes, top = expert_ids.shape[1], expert_ids.shape[-1]
    count = lax.axis_size("expert")
    peers = count // (GROUP * HALVES)
    part = width // GROUP
    block = GROUP * rows_dev
    same_expert, same_row, same_slice = groups(count)
    place = lax.axis_index("expert")
    half = place // GROUP % HALVES

    facts = [expert_ids[0].astype(jnp.bfloat16)] + in_three(route_gates[0])
    facts = jnp.stack(facts).transpose(2, 0, 1, 3).reshape(rows_dev, -1)
    facts = jnp.pad(facts, ((0, 0), (0, LANES - facts.shape[1])))
    sliced = hidden[0].reshape(rows_dev, GROUP, part).transpose(1, 0, 2)
    sliced = jnp.concatenate(
        [sliced, jnp.broadcast_to(facts[None], (GROUP, rows_dev, LANES))], axis=2
    )
    arrived = exchange(jnp.concatenate([sliced, sliced]), same_row)
    arrived = arrived.reshape(HALVES, block, part + LANES)
    arrived = lax.dynamic_slice_in_dim(jnp.concatenate([arrived, arrived]), half, HALVES, 0)
    arrived = arrived.reshape(HALVES * block, part + LANES)
    rows = arrived[:, :part]
    facts = arrived[:, part:].astype(jnp.float32)
    routes = facts[:, : 4 * passes * top].reshape(HALVES * block, 4, passes, top)

    up_slices = w_up[0].reshape(GROUP, part, HID_DEV)
    up = gathered(up_slices, spread(up_slices, place), place)
    up = up.transpose(1, 0, 2).reshape(part, HID)
    down_slices = w_down[0].reshape(HID_DEV, GROUP, part).transpose(1, 0, 2)
    gain = lax.dynamic_slice_in_dim(norm_gain[0], place % GROUP * part, part, 0)

    for t in range(passes):
        ids = routes[:, 0, t].astype(jnp.int32)
        gates = jnp.sum(routes[:, 1:, t], axis=1)
        picker, weigher = tables(ids, gates, half, peers, rows_dev)
        slots = jnp.dot(picker, rows, preferred_element_type=jnp.float32).astype(jnp.bfloat16)
        slots = exchange(slots, same_slice)
        if t == 0:
            slots, down_slices = lax.optimization_barrier((slots, down_slices))
            came = spread(down_slices, place)
        values = slots.astype(jnp.float32)
        squares = jnp.sum(values * values, axis=1)
        partial = jnp.dot(
            (values * gain).astype(jnp.bfloat16), up, preferred_element_type=jnp.float32
        ).astype(jnp.bfloat16)
        held = slots.shape[0]
        partial = partial.reshape(held, GROUP, HID_DEV).transpose(1, 0, 2)
        big = head(squares)
        beside = jnp.stack([big, squares - big]).astype(jnp.bfloat16).reshape(-1, LANES)
        beside = jnp.pad(beside, ((0, 16 - beside.shape[0]), (0, 0)))
        beside = jnp.broadcast_to(beside[None], (GROUP, 16, LANES))
        sums = jnp.sum(
            exchange(jnp.concatenate([partial, beside], axis=1), same_expert).astype(jnp.float32),
            axis=0,
        )
        squares = jnp.sum(sums[held:].reshape(-1)[: 2 * held].reshape(2, held), axis=0)
        scale = lax.rsqrt(squares / width + 1e-06)
        active = jax.nn.silu(sums[:held] * scale[:, None]).astype(jnp.bfloat16)
        active = lax.all_gather(active, "expert", axis_index_groups=same_expert)
        if t == 0:
            active, came = lax.optimization_barrier((active, came))
            down = gathered(down_slices, came, place).reshape(HID, part)
        active = active.transpose(1, 0, 2).reshape(held, HID)
        outputs = jnp.dot(active, down, preferred_element_type=jnp.float32).astype(jnp.bfloat16)
        outputs = exchange(outputs, same_slice)
        mixture = jnp.dot(
            weigher.T,
            outputs.astype(jnp.float32),
            precision=lax.Precision.HIGHEST,
            preferred_element_type=jnp.float32,
        )
        own = mixture[:block].astype(jnp.bfloat16)
        other = rows[block:].astype(jnp.float32) + mixture[block:]
        if t + 1 < passes:
            other = (other + other_half(own).astype(jnp.float32)).astype(jnp.bfloat16)
            own = next_section(other)
            rows = jnp.concatenate([own, other_half(own)])
        else:
            other = other.astype(jnp.bfloat16)
            both = lax.dynamic_slice_in_dim(jnp.stack([other, own, other]), half, HALVES, 0)
            both = exchange(both.reshape(HALVES * GROUP, rows_dev, part), same_row)
            both = both.reshape(HALVES, GROUP, rows_dev, part).astype(jnp.float32)
            done = jnp.sum(both, axis=0).astype(jnp.bfloat16)
            done = next_section(done.transpose(1, 0, 2).reshape(rows_dev, width))
    return done[None]


def solution(mesh):
    placed = (
        P("section", "expert", None),
        P("section", None),
        P("section", None, "expert"),
        P("section", "expert", None),
        P("section", None, "expert", None),
        P("section", None, "expert", None),
    )
    return jax.shard_map(
        body, mesh=mesh, in_specs=placed, out_specs=P("section", "expert", None), check_vma=False
    )
```

```python
import jax
import jax.numpy as jnp
from jax import lax
from jax.sharding import PartitionSpec as P

HID = 1024
HID_DEV = 128
GROUP = HID // HID_DEV
CAP = 4
HALVES = 2
LANES = 128


def groups(count):
    span = GROUP * HALVES
    same_expert = [[first + j for j in range(GROUP)] for first in range(0, count, GROUP)]
    same_row = [[first + k for k in range(span)] for first in range(0, count, span)]
    same_slice = [[first + k for first in range(0, count, span)] for k in range(span)]
    return same_expert, same_row, same_slice


def exchange(value, within):
    return lax.all_to_all(
        value, "expert", split_axis=0, concat_axis=0, axis_index_groups=within, tiled=True
    )


def other_half(value):
    count = lax.axis_size("expert")
    return lax.ppermute(value, "expert", [(i, i ^ GROUP) for i in range(count)])


def next_section(value):
    sections, count = lax.axis_size("section"), lax.axis_size("expert")
    route = [
        (s * count + i, (s + 1) % sections * count + (i ^ GROUP))
        for s in range(sections)
        for i in range(count)
    ]
    return lax.ppermute(value, ("section", "expert"), route)


def spread(slices, place):
    count = lax.axis_size("expert")
    return [
        lax.ppermute(
            lax.dynamic_index_in_dim(slices, place % GROUP ^ step, 0),
            "expert",
            [(i, i ^ step) for i in range(count)],
        )
        for step in range(1, GROUP)
    ]


def gathered(slices, came, place):
    for step in range(1, GROUP):
        slices = lax.dynamic_update_slice_in_dim(
            slices, came[step - 1], place % GROUP ^ step, 0
        )
    return slices


def paired(slices, place):
    count = lax.axis_size("expert")
    core = place % 2
    slices = slices.reshape((GROUP // 2, 2) + slices.shape[1:])
    keep = lax.dynamic_index_in_dim(slices, core, 1, keepdims=False)
    give = lax.dynamic_index_in_dim(slices, 1 - core, 1, keepdims=False)
    got = lax.ppermute(give, "expert", [(i, i ^ 1) for i in range(count)])
    return lax.dynamic_slice_in_dim(jnp.stack([keep, got, keep], axis=1), core, 2, 1)


def chips_spread(pair, place):
    count = lax.axis_size("expert")
    chip = place // 2 % (GROUP // 2)
    return [
        lax.ppermute(
            lax.dynamic_index_in_dim(pair, chip ^ step, 0),
            "expert",
            [(i, i ^ 2 * step) for i in range(count)],
        )
        for step in range(1, GROUP // 2)
    ]


def chips_gathered(pair, came, place):
    chip = place // 2 % (GROUP // 2)
    for step in range(1, GROUP // 2):
        pair = lax.dynamic_update_slice_in_dim(pair, came[step - 1], chip ^ step, 0)
    return pair


def head(value):
    return lax.reduce_precision(value, exponent_bits=8, mantissa_bits=7)


def in_three(value):
    first = head(value)
    second = head(value - first)
    third = head(value - first - second)
    return [part.astype(jnp.bfloat16) for part in (first, second, third)]


def tables(ids, gates, half, peers, rows_dev):
    rows = ids.shape[0]
    wanted = 2 * jnp.arange(peers, dtype=jnp.int32) + half
    hit = ids.T[None, :, :] == wanted[:, None, None]
    routed = jnp.any(hit, axis=1)
    weight = jnp.sum(jnp.where(hit, gates.T[None, :, :], 0.0), axis=1)
    at = jnp.arange(rows, dtype=jnp.int32)
    before = (at[:, None] < at[None, :]) & (at[:, None] // rows_dev == at[None, :] // rows_dev)
    rank = jnp.dot(
        routed.astype(jnp.bfloat16), before.astype(jnp.bfloat16), preferred_element_type=jnp.float32
    ).astype(jnp.int32)
    slots = rows // rows_dev * CAP
    slot = jnp.arange(slots, dtype=jnp.int32)
    mine = (slot[:, None] // CAP == at[None, :] // rows_dev)[None]
    picked = mine & routed[:, None, :] & (rank[:, None, :] == (slot % CAP)[None, :, None])
    weigher = jnp.where(picked, weight[:, None, :], 0.0)
    shape = (peers * slots, rows)
    return picked.astype(jnp.bfloat16).reshape(shape), weigher.reshape(shape)


def body(hidden, norm_gain, w_up, w_down, expert_ids, route_gates):
    width = hidden.shape[-1]
    rows_dev = hidden.shape[1]
    passes, top = expert_ids.shape[1], expert_ids.shape[-1]
    count = lax.axis_size("expert")
    peers = count // (GROUP * HALVES)
    part = width // GROUP
    block = GROUP * rows_dev
    same_expert, same_row, same_slice = groups(count)
    place = lax.axis_index("expert")
    half = place // GROUP % HALVES

    facts = [expert_ids[0].astype(jnp.bfloat16)] + in_three(route_gates[0])
    facts = jnp.stack(facts).transpose(2, 0, 1, 3).reshape(rows_dev, -1)
    facts = jnp.pad(facts, ((0, 0), (0, LANES - facts.shape[1])))
    sliced = hidden[0].reshape(rows_dev, GROUP, part).transpose(1, 0, 2)
    sliced = jnp.concatenate(
        [sliced, jnp.broadcast_to(facts[None], (GROUP, rows_dev, LANES))], axis=2
    )
    arrived = exchange(jnp.concatenate([sliced, sliced]), same_row)
    arrived, down_rows = lax.optimization_barrier((arrived, w_down[0]))
    arrived = arrived.reshape(HALVES, block, part + LANES)
    arrived = lax.dynamic_slice_in_dim(jnp.concatenate([arrived, arrived]), half, HALVES, 0)
    arrived = arrived.reshape(HALVES * block, part + LANES)
    rows = arrived[:, :part]
    facts = arrived[:, part:].astype(jnp.float32)
    routes = facts[:, : 4 * passes * top].reshape(HALVES * block, 4, passes, top)

    up_slices = w_up[0].reshape(GROUP, part, HID_DEV)
    up_came = spread(up_slices, place)
    down_pair = paired(down_rows.reshape(HID_DEV, GROUP, part).transpose(1, 0, 2), place)
    gain = lax.dynamic_slice_in_dim(norm_gain[0], place % GROUP * part, part, 0)

    for t in range(passes):
        ids = routes[:, 0, t].astype(jnp.int32)
        gates = jnp.sum(routes[:, 1:, t], axis=1)
        picker, weigher = tables(ids, gates, half, peers, rows_dev)
        slots = jnp.dot(picker, rows, preferred_element_type=jnp.float32).astype(jnp.bfloat16)
        slots = exchange(slots, same_slice)
        if t == 0:
            slots, up_came, down_pair = lax.optimization_barrier((slots, up_came, down_pair))
            down_came = chips_spread(down_pair, place)
            up = gathered(up_slices, up_came, place)
            up = up.transpose(1, 0, 2).reshape(part, HID)
        values = slots.astype(jnp.float32)
        squares = jnp.sum(values * values, axis=1)
        partial = jnp.dot(
            (values * gain).astype(jnp.bfloat16), up, preferred_element_type=jnp.float32
        ).astype(jnp.bfloat16)
        held = slots.shape[0]
        partial = partial.reshape(held, GROUP, HID_DEV).transpose(1, 0, 2)
        big = head(squares)
        beside = jnp.stack([big, squares - big]).astype(jnp.bfloat16).reshape(-1, LANES)
        beside = jnp.pad(beside, ((0, 16 - beside.shape[0]), (0, 0)))
        beside = jnp.broadcast_to(beside[None], (GROUP, 16, LANES))
        sums = jnp.sum(
            exchange(jnp.concatenate([partial, beside], axis=1), same_expert).astype(jnp.float32),
            axis=0,
        )
        squares = jnp.sum(sums[held:].reshape(-1)[: 2 * held].reshape(2, held), axis=0)
        scale = lax.rsqrt(squares / width + 1e-06)
        active = jax.nn.silu(sums[:held] * scale[:, None]).astype(jnp.bfloat16)
        active = lax.all_gather(active, "expert", axis_index_groups=same_expert)
        if t == 0:
            active, down_came = lax.optimization_barrier((active, down_came))
            down = chips_gathered(down_pair, down_came, place).reshape(HID, part)
        active = active.transpose(1, 0, 2).reshape(held, HID)
        outputs = jnp.dot(active, down, preferred_element_type=jnp.float32).astype(jnp.bfloat16)
        outputs = exchange(outputs, same_slice)
        mixture = jnp.dot(
            weigher.T,
            outputs.astype(jnp.float32),
            precision=lax.Precision.HIGHEST,
            preferred_element_type=jnp.float32,
        )
        own = mixture[:block].astype(jnp.bfloat16)
        other = rows[block:].astype(jnp.float32) + mixture[block:]
        if t + 1 < passes:
            other = (other + other_half(own).astype(jnp.float32)).astype(jnp.bfloat16)
            own = next_section(other)
            rows = jnp.concatenate([own, other_half(own)])
        else:
            other = other.astype(jnp.bfloat16)
            both = lax.dynamic_slice_in_dim(jnp.stack([other, own, other]), half, HALVES, 0)
            both = exchange(both.reshape(HALVES * GROUP, rows_dev, part), same_row)
            both = both.reshape(HALVES, GROUP, rows_dev, part).astype(jnp.float32)
            done = jnp.sum(both, axis=0).astype(jnp.bfloat16)
            done = next_section(done.transpose(1, 0, 2).reshape(rows_dev, width))
    return done[None]


def solution(mesh):
    placed = (
        P("section", "expert", None),
        P("section", None),
        P("section", None, "expert"),
        P("section", "expert", None),
        P("section", None, "expert", None),
        P("section", None, "expert", None),
    )
    return jax.shard_map(
        body, mesh=mesh, in_specs=placed, out_specs=P("section", "expert", None), check_vma=False
    )
```

```python
import jax
import jax.numpy as jnp
from jax import lax
from jax.sharding import PartitionSpec as P

HID = 1024
HID_DEV = 128
GROUP = HID // HID_DEV
PAIR = 4
CAP = 4
HALVES = 2
LANES = 128


def groups(count):
    span = GROUP * HALVES
    same_row = [[first + k for k in range(span)] for first in range(0, count, span)]
    same_place = [[first + k for first in range(0, count, span)] for k in range(span)]
    return same_row, same_place


def exchange(value, within):
    return lax.all_to_all(
        value, "expert", split_axis=0, concat_axis=0, axis_index_groups=within, tiled=True
    )


def swap(value, bit):
    count = lax.axis_size("expert")
    return lax.ppermute(value, "expert", [(i, i ^ bit) for i in range(count)])


def next_section(value):
    sections, count = lax.axis_size("section"), lax.axis_size("expert")
    route = [
        (s * count + i, (s + 1) % sections * count + (i ^ GROUP))
        for s in range(sections)
        for i in range(count)
    ]
    return lax.ppermute(value, ("section", "expert"), route)


def head(value):
    return lax.reduce_precision(value, exponent_bits=8, mantissa_bits=7)


def in_three(value):
    first = head(value)
    second = head(value - first)
    third = head(value - first - second)
    return [part.astype(jnp.bfloat16) for part in (first, second, third)]


def take(value, index, axis):
    return lax.dynamic_index_in_dim(value, index, axis, keepdims=False)


def recut(quarters, chip, core):
    near = swap(take(quarters, 1 - core, 1), 1)
    both = jnp.stack([take(quarters, core, 1), near], axis=1)
    far = swap(take(both, 1 - chip, 0), 2)
    return take(both, chip, 0), far


def tables(ids, gates, half, peers, rows_dev):
    rows = ids.shape[0]
    wanted = 2 * jnp.arange(peers, dtype=jnp.int32) + half
    hit = ids.T[None, :, :] == wanted[:, None, None]
    routed = jnp.any(hit, axis=1)
    weight = jnp.sum(jnp.where(hit, gates.T[None, :, :], 0.0), axis=1)
    at = jnp.arange(rows, dtype=jnp.int32)
    before = (at[:, None] < at[None, :]) & (at[:, None] // rows_dev == at[None, :] // rows_dev)
    rank = jnp.dot(
        routed.astype(jnp.bfloat16), before.astype(jnp.bfloat16), preferred_element_type=jnp.float32
    ).astype(jnp.int32)
    slots = rows // rows_dev * CAP
    slot = jnp.arange(slots, dtype=jnp.int32)
    mine = (slot[:, None] // CAP == at[None, :] // rows_dev)[None]
    picked = mine & routed[:, None, :] & (rank[:, None, :] == (slot % CAP)[None, :, None])
    weigher = jnp.where(picked, weight[:, None, :], 0.0)
    shape = (peers * slots, rows)
    return picked.astype(jnp.bfloat16).reshape(shape), weigher.reshape(shape)


def body(hidden, norm_gain, w_up, w_down, expert_ids, route_gates):
    width = hidden.shape[-1]
    rows_dev = hidden.shape[1]
    passes, top = expert_ids.shape[1], expert_ids.shape[-1]
    count = lax.axis_size("expert")
    peers = count // (GROUP * HALVES)
    part = width // PAIR
    piece = part // 2
    block = GROUP * rows_dev
    same_row, same_place = groups(count)
    place = lax.axis_index("expert")
    core, chip, pair, half = place % 2, place // 2 % 2, place // 4 % 2, place // 8 % 2

    facts = [expert_ids[0].astype(jnp.bfloat16)] + in_three(route_gates[0])
    facts = jnp.stack(facts).transpose(2, 0, 1, 3).reshape(rows_dev, -1)
    facts = jnp.pad(facts, ((0, 0), (0, LANES - facts.shape[1])))
    quarters = hidden[0].reshape(rows_dev, PAIR, part).transpose(1, 0, 2)
    quarters = jnp.concatenate(
        [quarters, jnp.broadcast_to(facts[None], (PAIR, rows_dev, LANES))], axis=2
    )
    sent, w_up, w_down = lax.optimization_barrier(
        (jnp.concatenate([quarters] * (2 * HALVES)), w_up, w_down)
    )
    arrived = exchange(sent, same_row)
    up, up_far = recut(w_up[0].reshape(2, 2, part, HID_DEV), chip, core)
    down, down_far = recut(w_down[0].reshape(HID_DEV, 2, 2, part).transpose(1, 2, 0, 3), chip, core)
    arrived, up, up_far, down = lax.optimization_barrier((arrived, up, up_far, down))
    arrived = arrived.reshape(HALVES, block, part + LANES)
    arrived = lax.dynamic_slice_in_dim(jnp.concatenate([arrived, arrived]), half, HALVES, 0)
    arrived = arrived.reshape(HALVES * block, part + LANES)
    rows = arrived[:, :part]
    facts = arrived[:, part:].astype(jnp.float32)
    routes = facts[:, : 4 * passes * top].reshape(HALVES * block, 4, passes, top)

    up = [up[0], up[1], up_far[0], up_far[1]]
    gain = lax.dynamic_slice_in_dim(norm_gain[0], place % PAIR * part, part, 0)

    for t in range(passes):
        ids = routes[:, 0, t].astype(jnp.int32)
        gates = jnp.sum(routes[:, 1:, t], axis=1)
        picker, weigher = tables(ids, gates, half, peers, rows_dev)
        slots = jnp.dot(picker, rows, preferred_element_type=jnp.float32).astype(jnp.bfloat16)
        slots = exchange(slots, same_place)
        if t == 0:
            slots, down_far = lax.optimization_barrier((slots, down_far))
            down = jnp.concatenate([down, down_far]).reshape(PAIR * HID_DEV, part)
        values = slots.astype(jnp.float32)
        squares = jnp.broadcast_to(
            jnp.sum(values * values, axis=1, keepdims=True), (slots.shape[0], LANES)
        )
        scaled = (values * gain).astype(jnp.bfloat16)
        sums = [
            jnp.dot(scaled, up[k], preferred_element_type=jnp.float32) for k in range(PAIR)
        ]
        came = swap(jnp.stack([sums[1], sums[3], squares]), 1)
        sums = [sums[0] + came[0], sums[2] + came[1]]
        squares = squares + came[2]
        came = swap(jnp.stack([sums[1], squares]), 2)
        scale = lax.rsqrt((squares + came[1]) / width + 1e-06)
        active = jax.nn.silu((sums[0] + came[0]) * scale).astype(jnp.bfloat16)
        active = jnp.stack([active, swap(active, 1)])
        active = jnp.concatenate([active, swap(active, 2)])
        active = jnp.concatenate([active[k] for k in range(PAIR)], axis=1)
        outputs = jnp.dot(active, down, preferred_element_type=jnp.float32).astype(jnp.bfloat16)
        outputs = exchange(outputs, same_place)
        mixture = jnp.dot(
            weigher.T,
            outputs.astype(jnp.float32),
            precision=lax.Precision.HIGHEST,
            preferred_element_type=jnp.float32,
        )
        if t + 1 < passes:
            mixture = mixture.reshape(2 * block, 2, piece)
            mine = take(mixture, pair, 1)
            mine = mine + swap(take(mixture, 1 - pair, 1).astype(jnp.bfloat16), 4).astype(
                jnp.float32
            )
            kept = take(rows[block:].reshape(block, 2, piece), pair, 1).astype(jnp.float32)
            other = swap(mine[:block].astype(jnp.bfloat16), 8).astype(jnp.float32)
            own = next_section((kept + mine[block:] + other).astype(jnp.bfloat16))
            rows = jnp.concatenate([own, swap(own, 8)])
            pieces = jnp.stack([rows, swap(rows, 4), rows], axis=1)
            rows = lax.dynamic_slice_in_dim(pieces, pair, 2, 1).reshape(2 * block, part)
        else:
            own = mixture[:block].astype(jnp.bfloat16)
            kept = jnp.where(pair == 0, rows[block:].astype(jnp.float32), 0.0)
            other = (kept + mixture[block:]).astype(jnp.bfloat16)
            both = lax.dynamic_slice_in_dim(jnp.stack([other, own, other]), half, HALVES, 0)
            both = exchange(both.reshape(HALVES * GROUP, rows_dev, part), same_row)
            both = both.reshape(2 * HALVES, PAIR, rows_dev, part).astype(jnp.float32)
            done = jnp.sum(both, axis=0).astype(jnp.bfloat16)
            done = next_section(done.transpose(1, 0, 2).reshape(rows_dev, width))
    return done[None]


def solution(mesh):
    placed = (
        P("section", "expert", None),
        P("section", None),
        P("section", None, "expert"),
        P("section", "expert", None),
        P("section", None, "expert", None),
        P("section", None, "expert", None),
    )
    return jax.shard_map(
        body, mesh=mesh, in_specs=placed, out_specs=P("section", "expert", None), check_vma=False
    )
```

```python
import jax
import jax.numpy as jnp
from jax import lax
from jax.sharding import PartitionSpec as P

HID = 1024
HID_DEV = 128
GROUP = HID // HID_DEV
PAIR = 4
CAP = 4
HALVES = 2
LANES = 128
SIDE = 4


def groups(count):
    span = GROUP * HALVES
    same_row = [[first + k for k in range(span)] for first in range(0, count, span)]
    same_place = [[first + k for first in range(0, count, span)] for k in range(span)]
    same_quarter = [
        [first + k for k in range(q, span, PAIR)]
        for first in range(0, count, span)
        for q in range(PAIR)
    ]
    return same_row, same_place, same_quarter


def exchange(value, within):
    return lax.all_to_all(
        value, "expert", split_axis=0, concat_axis=0, axis_index_groups=within, tiled=True
    )


def swap(value, bit):
    count = lax.axis_size("expert")
    return lax.ppermute(value, "expert", [(i, i ^ bit) for i in range(count)])


def next_section(value):
    sections, count = lax.axis_size("section"), lax.axis_size("expert")
    route = [
        (s * count + i, (s + 1) % sections * count + (i ^ GROUP if s % SIDE == SIDE - 1 else i))
        for s in range(sections)
        for i in range(count)
    ]
    return lax.ppermute(value, ("section", "expert"), route)


def head(value):
    return lax.reduce_precision(value, exponent_bits=8, mantissa_bits=7)


def in_three(value):
    first = head(value)
    second = head(value - first)
    third = head(value - first - second)
    return [part.astype(jnp.bfloat16) for part in (first, second, third)]


def take(value, index, axis):
    return lax.dynamic_index_in_dim(value, index, axis, keepdims=False)


def recut(quarters, chip, core):
    near = swap(take(quarters, 1 - core, 1), 1)
    both = jnp.stack([take(quarters, core, 1), near], axis=1)
    far = swap(take(both, 1 - chip, 0), 2)
    return take(both, chip, 0), far


def tables(ids, gates, half, peers, rows_dev):
    rows = ids.shape[0]
    wanted = 2 * jnp.arange(peers, dtype=jnp.int32) + half
    hit = ids.T[None, :, :] == wanted[:, None, None]
    routed = jnp.any(hit, axis=1)
    weight = jnp.sum(jnp.where(hit, gates.T[None, :, :], 0.0), axis=1)
    at = jnp.arange(rows, dtype=jnp.int32)
    before = (at[:, None] < at[None, :]) & (at[:, None] // rows_dev == at[None, :] // rows_dev)
    rank = jnp.dot(
        routed.astype(jnp.bfloat16), before.astype(jnp.bfloat16), preferred_element_type=jnp.float32
    ).astype(jnp.int32)
    slots = rows // rows_dev * CAP
    slot = jnp.arange(slots, dtype=jnp.int32)
    mine = (slot[:, None] // CAP == at[None, :] // rows_dev)[None]
    picked = mine & routed[:, None, :] & (rank[:, None, :] == (slot % CAP)[None, :, None])
    weigher = jnp.where(picked, weight[:, None, :], 0.0)
    shape = (peers * slots, rows)
    return picked.astype(jnp.bfloat16).reshape(shape), weigher.reshape(shape)


def body(hidden, norm_gain, w_up, w_down, expert_ids, route_gates):
    width = hidden.shape[-1]
    rows_dev = hidden.shape[1]
    passes, top = expert_ids.shape[1], expert_ids.shape[-1]
    count = lax.axis_size("expert")
    peers = count // (GROUP * HALVES)
    part = width // PAIR
    piece = part // 2
    block = GROUP * rows_dev
    same_row, same_place, same_quarter = groups(count)
    place = lax.axis_index("expert")
    core, chip, pair, half = place % 2, place // 2 % 2, place // 4 % 2, place // 8 % 2
    crosses = (lax.axis_index("section") % SIDE == SIDE - 1).astype(jnp.int32)

    facts = [expert_ids[0].astype(jnp.bfloat16)] + in_three(route_gates[0])
    facts = jnp.stack(facts).transpose(2, 0, 1, 3).reshape(rows_dev, -1)
    facts = jnp.pad(facts, ((0, 0), (0, LANES - facts.shape[1])))
    quarters = hidden[0].reshape(rows_dev, PAIR, part).transpose(1, 0, 2)
    quarters = jnp.concatenate(
        [quarters, jnp.broadcast_to(facts[None], (PAIR, rows_dev, LANES))], axis=2
    )
    sent, w_up, w_down = lax.optimization_barrier(
        (jnp.concatenate([quarters] * (2 * HALVES)), w_up, w_down)
    )
    arrived = exchange(sent, same_row)
    up, up_far = recut(w_up[0].reshape(2, 2, part, HID_DEV), chip, core)
    down, down_far = recut(w_down[0].reshape(HID_DEV, 2, 2, part).transpose(1, 2, 0, 3), chip, core)
    arrived, up, up_far, down = lax.optimization_barrier((arrived, up, up_far, down))
    arrived = arrived.reshape(HALVES, block, part + LANES)
    arrived = lax.dynamic_slice_in_dim(jnp.concatenate([arrived, arrived]), half, HALVES, 0)
    arrived = arrived.reshape(HALVES * block, part + LANES)
    rows = arrived[:, :part]
    facts = arrived[:, part:].astype(jnp.float32)
    routes = facts[:, : 4 * passes * top].reshape(HALVES * block, 4, passes, top)

    up = [up[0], up[1], up_far[0], up_far[1]]
    gain = lax.dynamic_slice_in_dim(norm_gain[0], place % PAIR * part, part, 0)

    for t in range(passes):
        ids = routes[:, 0, t].astype(jnp.int32)
        gates = jnp.sum(routes[:, 1:, t], axis=1)
        picker, weigher = tables(ids, gates, half, peers, rows_dev)
        slots = jnp.dot(picker, rows, preferred_element_type=jnp.float32).astype(jnp.bfloat16)
        slots = exchange(slots, same_place)
        if t == 0:
            slots, down_far = lax.optimization_barrier((slots, down_far))
            down = jnp.concatenate([down, down_far]).reshape(PAIR * HID_DEV, part)
        values = slots.astype(jnp.float32)
        squares = jnp.broadcast_to(
            jnp.sum(values * values, axis=1, keepdims=True), (slots.shape[0], LANES)
        )
        scaled = (values * gain).astype(jnp.bfloat16)
        sums = [
            jnp.dot(scaled, up[k], preferred_element_type=jnp.float32) for k in range(PAIR)
        ]
        came = swap(jnp.stack([sums[1], sums[3], squares]), 1)
        sums = [sums[0] + came[0], sums[2] + came[1]]
        squares = squares + came[2]
        came = swap(jnp.stack([sums[1], squares]), 2)
        scale = lax.rsqrt((squares + came[1]) / width + 1e-06)
        active = jax.nn.silu((sums[0] + came[0]) * scale).astype(jnp.bfloat16)
        active = jnp.stack([active, swap(active, 1)])
        active = jnp.concatenate([active, swap(active, 2)])
        active = jnp.concatenate([active[k] for k in range(PAIR)], axis=1)
        outputs = jnp.dot(active, down, preferred_element_type=jnp.float32).astype(jnp.bfloat16)
        outputs = exchange(outputs, same_place)
        mixture = jnp.dot(
            weigher.T,
            outputs.astype(jnp.float32),
            precision=lax.Precision.HIGHEST,
            preferred_element_type=jnp.float32,
        )
        mixture = mixture.reshape(HALVES, block, part)
        if t + 1 < passes:
            sent = mixture.astype(jnp.bfloat16).reshape(HALVES, block, 2, piece)
            sent = jnp.concatenate([sent, sent[:1]])
            sent = lax.dynamic_slice_in_dim(sent, half ^ crosses, HALVES, 0)
            sent = sent.transpose(0, 2, 1, 3).reshape(2 * HALVES, block, piece)
            came = exchange(sent, same_quarter).astype(jnp.float32)
            kept = take(rows.reshape(HALVES, block, 2, piece), crosses, 0)
            kept = take(kept, pair, 1).astype(jnp.float32)
            own = next_section((kept + jnp.sum(came, axis=0)).astype(jnp.bfloat16))
            rows = jnp.concatenate([own, swap(own, 8)])
            pieces = jnp.stack([rows, swap(rows, 4), rows], axis=1)
            rows = lax.dynamic_slice_in_dim(pieces, pair, 2, 1).reshape(2 * block, part)
        else:
            kept = jnp.where(pair == 0, rows[block:].astype(jnp.float32), 0.0)
            own = mixture[0].astype(jnp.bfloat16)
            other = (kept + mixture[1]).astype(jnp.bfloat16)
            both = jnp.stack([own, other, own])
            both = lax.dynamic_slice_in_dim(both, half ^ crosses, HALVES, 0)
            both = exchange(both.reshape(HALVES * GROUP, rows_dev, part), same_row)
            both = both.reshape(2 * HALVES, PAIR, rows_dev, part).astype(jnp.float32)
            done = jnp.sum(both, axis=0).astype(jnp.bfloat16)
            done = next_section(done.transpose(1, 0, 2).reshape(rows_dev, width))
    return done[None]


def solution(mesh):
    placed = (
        P("section", "expert", None),
        P("section", None),
        P("section", None, "expert"),
        P("section", "expert", None),
        P("section", None, "expert", None),
        P("section", None, "expert", None),
    )
    return jax.shard_map(
        body, mesh=mesh, in_specs=placed, out_specs=P("section", "expert", None), check_vma=False
    )
```

```python
import jax
import jax.numpy as jnp
from jax import lax
from jax.sharding import PartitionSpec as P

HID = 1024
HID_DEV = 128
GROUP = HID // HID_DEV
PAIR = 4
CAP = 4
HALVES = 2
LANES = 128


def groups(count):
    span = GROUP * HALVES
    same_row = [[first + k for k in range(span)] for first in range(0, count, span)]
    same_place = [[first + k for first in range(0, count, span)] for k in range(span)]
    return same_row, same_place


def exchange(value, within):
    return lax.all_to_all(
        value, "expert", split_axis=0, concat_axis=0, axis_index_groups=within, tiled=True
    )


def swap(value, bit):
    count = lax.axis_size("expert")
    return lax.ppermute(value, "expert", [(i, i ^ bit) for i in range(count)])


def next_section(value):
    sections, count = lax.axis_size("section"), lax.axis_size("expert")
    route = [
        (s * count + i, (s + 1) % sections * count + (i ^ GROUP))
        for s in range(sections)
        for i in range(count)
    ]
    return lax.ppermute(value, ("section", "expert"), route)


def head(value):
    return lax.reduce_precision(value, exponent_bits=8, mantissa_bits=7)


def in_three(value):
    first = head(value)
    second = head(value - first)
    third = head(value - first - second)
    return [part.astype(jnp.bfloat16) for part in (first, second, third)]


def take(value, index, axis):
    return lax.dynamic_index_in_dim(value, index, axis, keepdims=False)


def recut(quarters, chip, core):
    near = swap(take(quarters, 1 - core, 1), 1)
    both = jnp.stack([take(quarters, core, 1), near], axis=1)
    far = swap(take(both, 1 - chip, 0), 2)
    return take(both, chip, 0), far


def tables(ids, gates, half, peers, rows_dev):
    rows = ids.shape[0]
    wanted = 2 * jnp.arange(peers, dtype=jnp.int32) + half
    hit = ids.T[None, :, :] == wanted[:, None, None]
    routed = jnp.any(hit, axis=1)
    weight = jnp.sum(jnp.where(hit, gates.T[None, :, :], 0.0), axis=1)
    at = jnp.arange(rows, dtype=jnp.int32)
    before = (at[:, None] < at[None, :]) & (at[:, None] // rows_dev == at[None, :] // rows_dev)
    rank = jnp.dot(
        routed.astype(jnp.bfloat16), before.astype(jnp.bfloat16), preferred_element_type=jnp.float32
    ).astype(jnp.int32)
    slots = rows // rows_dev * CAP
    slot = jnp.arange(slots, dtype=jnp.int32)
    mine = (slot[:, None] // CAP == at[None, :] // rows_dev)[None]
    picked = mine & routed[:, None, :] & (rank[:, None, :] == (slot % CAP)[None, :, None])
    weigher = jnp.where(picked, weight[:, None, :], 0.0)
    return picked.astype(jnp.bfloat16), weigher


def pick(picker, rows):
    return lax.dot_general(
        picker, rows, (((2,), (0,)), ((), ())), preferred_element_type=jnp.float32
    ).astype(jnp.bfloat16)


def mix(weigher, outputs):
    return jnp.dot(
        weigher.reshape(-1, weigher.shape[-1]).T,
        outputs.reshape(-1, outputs.shape[-1]).astype(jnp.float32),
        precision=lax.Precision.HIGHEST,
        preferred_element_type=jnp.float32,
    )


def whole_quarter(mine, other, pair):
    pieces = jnp.stack([mine, other, mine], axis=1)
    pieces = lax.dynamic_slice_in_dim(pieces, pair, 2, 1)
    return pieces.reshape(mine.shape[0], -1)


def body(hidden, norm_gain, w_up, w_down, expert_ids, route_gates):
    width = hidden.shape[-1]
    rows_dev = hidden.shape[1]
    passes, top = expert_ids.shape[1], expert_ids.shape[-1]
    count = lax.axis_size("expert")
    peers = count // (GROUP * HALVES)
    part = width // PAIR
    piece = part // 2
    block = GROUP * rows_dev
    same_row, same_place = groups(count)
    place = lax.axis_index("expert")
    core, chip, pair, half = place % 2, place // 2 % 2, place // 4 % 2, place // 8 % 2

    facts = [expert_ids[0].astype(jnp.bfloat16)] + in_three(route_gates[0])
    facts = jnp.stack(facts).transpose(2, 0, 1, 3).reshape(rows_dev, -1)
    facts = jnp.pad(facts, ((0, 0), (0, LANES - facts.shape[1])))
    quarters = hidden[0].reshape(rows_dev, PAIR, part).transpose(1, 0, 2)
    quarters = jnp.concatenate(
        [quarters, jnp.broadcast_to(facts[None], (PAIR, rows_dev, LANES))], axis=2
    )
    sent, w_up, w_down = lax.optimization_barrier(
        (jnp.concatenate([quarters] * (2 * HALVES)), w_up, w_down)
    )
    arrived = exchange(sent, same_row)
    up, up_far = recut(w_up[0].reshape(2, 2, part, HID_DEV), chip, core)
    down, down_far = recut(w_down[0].reshape(HID_DEV, 2, 2, part).transpose(1, 2, 0, 3), chip, core)
    arrived, up, up_far, down = lax.optimization_barrier((arrived, up, up_far, down))
    arrived = arrived.reshape(HALVES, block, part + LANES)
    arrived = lax.dynamic_slice_in_dim(jnp.concatenate([arrived, arrived]), half, HALVES, 0)
    own, other = arrived[0, :, :part], arrived[1, :, :part]
    facts = arrived[:, :, part:].astype(jnp.float32)
    routes = facts[:, :, : 4 * passes * top].reshape(HALVES, block, 4, passes, top)

    up = [up[0], up[1], up_far[0], up_far[1]]
    gain = lax.dynamic_slice_in_dim(norm_gain[0], place % PAIR * part, part, 0)

    for t in range(passes):
        ids = routes[:, :, 0, t].astype(jnp.int32)
        gates = jnp.sum(routes[:, :, 1:, t], axis=2)
        own_picker, own_weigher = tables(ids[0], gates[0], half, peers, rows_dev)
        other_picker, other_weigher = tables(ids[1], gates[1], half, peers, rows_dev)
        if t == 0:
            slots = jnp.concatenate([pick(own_picker, own), pick(other_picker, other)], axis=1)
            slots = exchange(slots, same_place)
        else:
            mine = next_section(mine)
            theirs = swap(mine, 8)
            own = whole_quarter(mine, swap(mine, 4), pair)
            own_slots = exchange(pick(own_picker, own), same_place)
            other = whole_quarter(theirs, swap(theirs, 4), pair)
            other_slots = exchange(pick(other_picker, other), same_place)
            slots = jnp.concatenate([own_slots, other_slots], axis=1)
        slots = slots.reshape(-1, part)
        if t == 0:
            slots, down_far = lax.optimization_barrier((slots, down_far))
            down = jnp.concatenate([down, down_far]).reshape(PAIR * HID_DEV, part)
        values = slots.astype(jnp.float32)
        squares = jnp.broadcast_to(
            jnp.sum(values * values, axis=1, keepdims=True), (slots.shape[0], LANES)
        )
        scaled = (values * gain).astype(jnp.bfloat16)
        sums = [
            jnp.dot(scaled, up[k], preferred_element_type=jnp.float32) for k in range(PAIR)
        ]
        came = swap(jnp.stack([sums[1], sums[3], squares]), 1)
        sums = [sums[0] + came[0], sums[2] + came[1]]
        squares = squares + came[2]
        came = swap(jnp.stack([sums[1], squares]), 2)
        scale = lax.rsqrt((squares + came[1]) / width + 1e-06)
        active = jax.nn.silu((sums[0] + came[0]) * scale).astype(jnp.bfloat16)
        active = jnp.stack([active, swap(active, 1)])
        active = jnp.concatenate([active, swap(active, 2)])
        active = jnp.concatenate([active[k] for k in range(PAIR)], axis=1)
        outputs = jnp.dot(active, down, preferred_element_type=jnp.float32).astype(jnp.bfloat16)
        outputs = outputs.reshape(peers, HALVES, -1, part)
        if t + 1 < passes:
            own_mix = mix(own_weigher, exchange(outputs[:, 0], same_place))
            crossed = swap(own_mix.astype(jnp.bfloat16), 8).astype(jnp.float32)
            other_mix = mix(other_weigher, exchange(outputs[:, 1], same_place)) + crossed
            other_mix = other_mix.reshape(block, 2, piece)
            given = swap(take(other_mix, 1 - pair, 1).astype(jnp.bfloat16), 4)
            kept = take(other.reshape(block, 2, piece), pair, 1).astype(jnp.float32)
            mine = kept + take(other_mix, pair, 1) + given.astype(jnp.float32)
            mine = mine.astype(jnp.bfloat16)
        else:
            outputs = exchange(outputs.reshape(peers, -1, part), same_place)
            outputs = outputs.reshape(peers, HALVES, -1, part)
            own_mix = mix(own_weigher, outputs[:, 0]).astype(jnp.bfloat16)
            kept = jnp.where(pair == 0, other.astype(jnp.float32), 0.0)
            other_mix = (kept + mix(other_weigher, outputs[:, 1])).astype(jnp.bfloat16)
            both = jnp.stack([other_mix, own_mix, other_mix])
            both = lax.dynamic_slice_in_dim(both, half, HALVES, 0)
            both = exchange(both.reshape(HALVES * GROUP, rows_dev, part), same_row)
            both = both.reshape(2 * HALVES, PAIR, rows_dev, part).astype(jnp.float32)
            done = jnp.sum(both, axis=0).astype(jnp.bfloat16)
            done = next_section(done.transpose(1, 0, 2).reshape(rows_dev, width))
    return done[None]


def solution(mesh):
    placed = (
        P("section", "expert", None),
        P("section", None),
        P("section", None, "expert"),
        P("section", "expert", None),
        P("section", None, "expert", None),
        P("section", None, "expert", None),
    )
    return jax.shard_map(
        body, mesh=mesh, in_specs=placed, out_specs=P("section", "expert", None), check_vma=False
    )
```

```python
import jax
import jax.numpy as jnp
from jax import lax
from jax.sharding import PartitionSpec as P

HID = 1024
HID_DEV = 128
GROUP = HID // HID_DEV
PAIR = 4
CAP = 4
HALVES = 2
LANES = 128


def groups(count):
    span = GROUP * HALVES
    same_row = [[first + k for k in range(span)] for first in range(0, count, span)]
    same_place = [[first + k for first in range(0, count, span)] for k in range(span)]
    return same_row, same_place


def exchange(value, within):
    return lax.all_to_all(
        value, "expert", split_axis=0, concat_axis=0, axis_index_groups=within, tiled=True
    )


def swap(value, bit):
    count = lax.axis_size("expert")
    return lax.ppermute(value, "expert", [(i, i ^ bit) for i in range(count)])


def next_section(value):
    sections, count = lax.axis_size("section"), lax.axis_size("expert")
    route = [
        (s * count + i, (s + 1) % sections * count + (i ^ GROUP))
        for s in range(sections)
        for i in range(count)
    ]
    return lax.ppermute(value, ("section", "expert"), route)


def head(value):
    return lax.reduce_precision(value, exponent_bits=8, mantissa_bits=7)


def in_three(value):
    first = head(value)
    second = head(value - first)
    third = head(value - first - second)
    return [part.astype(jnp.bfloat16) for part in (first, second, third)]


def take(value, index, axis):
    return lax.dynamic_index_in_dim(value, index, axis, keepdims=False)


def recut(quarters, chip, core):
    near = swap(take(quarters, 1 - core, 1), 1)
    both = jnp.stack([take(quarters, core, 1), near], axis=1)
    far = swap(take(both, 1 - chip, 0), 2)
    return take(both, chip, 0), far


def tables(ids, gates, half, peers, rows_dev):
    rows = ids.shape[0]
    wanted = 2 * jnp.arange(peers, dtype=jnp.int32) + half
    hit = ids.T[None, :, :] == wanted[:, None, None]
    routed = jnp.any(hit, axis=1)
    weight = jnp.sum(jnp.where(hit, gates.T[None, :, :], 0.0), axis=1)
    at = jnp.arange(rows, dtype=jnp.int32)
    before = (at[:, None] < at[None, :]) & (at[:, None] // rows_dev == at[None, :] // rows_dev)
    rank = jnp.dot(
        routed.astype(jnp.bfloat16), before.astype(jnp.bfloat16), preferred_element_type=jnp.float32
    ).astype(jnp.int32)
    slots = rows // rows_dev * CAP
    slot = jnp.arange(slots, dtype=jnp.int32)
    mine = (slot[:, None] // CAP == at[None, :] // rows_dev)[None]
    picked = mine & routed[:, None, :] & (rank[:, None, :] == (slot % CAP)[None, :, None])
    weigher = jnp.where(picked, weight[:, None, :], 0.0)
    shape = (peers * slots, rows)
    return picked.astype(jnp.bfloat16).reshape(shape), weigher.reshape(shape)


def normed_quarters(current, gain):
    values = current.astype(jnp.float32)
    inverse_rms = lax.rsqrt(jnp.mean(values * values, axis=-1, keepdims=True) + 1e-06)
    normed = (values * inverse_rms * gain).astype(jnp.bfloat16)
    return normed.reshape(current.shape[0], PAIR, -1).transpose(1, 0, 2)


def body(hidden, norm_gain, w_up, w_down, expert_ids, route_gates):
    width = hidden.shape[-1]
    rows_dev = hidden.shape[1]
    passes, top = expert_ids.shape[1], expert_ids.shape[-1]
    count = lax.axis_size("expert")
    peers = count // (GROUP * HALVES)
    part = width // PAIR
    block = GROUP * rows_dev
    total = HALVES * block
    same_row, same_place = groups(count)
    place = lax.axis_index("expert")
    core, chip, half = place % 2, place // 2 % 2, place // GROUP % HALVES
    gain = norm_gain[0]
    current = hidden[0]

    facts = [expert_ids[0].astype(jnp.bfloat16)] + in_three(route_gates[0])
    facts = jnp.stack(facts).transpose(2, 0, 1, 3).reshape(rows_dev, -1)
    facts = jnp.pad(facts, ((0, 0), (0, LANES - facts.shape[1])))

    for t in range(passes):
        sent = normed_quarters(current, gain)
        if t == 0:
            facts = jnp.broadcast_to(facts[None], (PAIR, rows_dev, LANES))
            sent = jnp.concatenate([sent, facts], axis=2)
        sent = jnp.concatenate([sent] * (2 * HALVES))
        if t == 0:
            sent, w_up, w_down = lax.optimization_barrier((sent, w_up, w_down))
        arrived = exchange(sent, same_row)
        if t == 0:
            up, up_far = recut(w_up[0].reshape(2, 2, part, HID_DEV), chip, core)
            down = w_down[0].reshape(HID_DEV, 2, 2, part).transpose(1, 2, 0, 3)
            down, down_far = recut(down, chip, core)
            arrived, up, up_far, down = lax.optimization_barrier((arrived, up, up_far, down))
            up = [up[0], up[1], up_far[0], up_far[1]]
            facts = arrived[:, :, part:].astype(jnp.float32).reshape(total, LANES)
            routes = facts[:, : 4 * passes * top].reshape(total, 4, passes, top)
            arrived = arrived[:, :, :part]
        rows = arrived.reshape(total, part)

        ids = routes[:, 0, t].astype(jnp.int32)
        gates = jnp.sum(routes[:, 1:, t], axis=1)
        picker, weigher = tables(ids, gates, half, peers, rows_dev)
        slots = jnp.dot(picker, rows, preferred_element_type=jnp.float32).astype(jnp.bfloat16)
        slots = exchange(slots, same_place)
        if t == 0:
            slots, down_far = lax.optimization_barrier((slots, down_far))
            down = jnp.concatenate([down, down_far]).reshape(PAIR * HID_DEV, part)
        sums = [jnp.dot(slots, up[k], preferred_element_type=jnp.float32) for k in range(PAIR)]
        came = swap(jnp.stack([sums[1], sums[3]]), 1)
        came_far = swap(sums[2] + came[1], 2)
        active = jax.nn.silu(sums[0] + came[0] + came_far).astype(jnp.bfloat16)
        active = jnp.stack([active, swap(active, 1)])
        active = jnp.concatenate([active, swap(active, 2)])
        active = jnp.concatenate([active[k] for k in range(PAIR)], axis=1)
        outputs = jnp.dot(active, down, preferred_element_type=jnp.float32).astype(jnp.bfloat16)
        outputs, current = lax.optimization_barrier((outputs, current))
        residual = swap(current, GROUP)
        outputs, residual = lax.optimization_barrier((exchange(outputs, same_place), residual))
        mixture = jnp.dot(
            weigher.T,
            outputs.astype(jnp.float32),
            precision=lax.Precision.HIGHEST,
            preferred_element_type=jnp.float32,
        )
        mixture = mixture.astype(jnp.bfloat16).reshape(HALVES, GROUP, rows_dev, part)
        mixture = jnp.concatenate([mixture[1], mixture[0]])
        came = exchange(mixture, same_row).reshape(2 * HALVES, PAIR, rows_dev, part)
        came = jnp.sum(came.astype(jnp.float32), axis=0).transpose(1, 0, 2)
        updated = residual.astype(jnp.float32) + came.reshape(rows_dev, width)
        current = next_section(updated.astype(jnp.bfloat16))
    return current[None]


def solution(mesh):
    placed = (
        P("section", "expert", None),
        P("section", None),
        P("section", None, "expert"),
        P("section", "expert", None),
        P("section", None, "expert", None),
        P("section", None, "expert", None),
    )
    return jax.shard_map(
        body, mesh=mesh, in_specs=placed, out_specs=P("section", "expert", None), check_vma=False
    )
```

```python
import jax
import jax.numpy as jnp
from jax import lax
from jax.sharding import PartitionSpec as P

HID = 1024
HID_DEV = 128
GROUP = HID // HID_DEV
PAIR = 4
CAP = 4
HALVES = 2
LANES = 128


def groups(count):
    span = GROUP * HALVES
    same_row = [[first + k for k in range(span)] for first in range(0, count, span)]
    same_place = [[first + k for first in range(0, count, span)] for k in range(span)]
    return same_row, same_place


def exchange(value, within):
    return lax.all_to_all(
        value, "expert", split_axis=0, concat_axis=0, axis_index_groups=within, tiled=True
    )


def swap(value, bit):
    count = lax.axis_size("expert")
    return lax.ppermute(value, "expert", [(i, i ^ bit) for i in range(count)])


def next_section(value):
    sections, count = lax.axis_size("section"), lax.axis_size("expert")
    route = [
        (s * count + i, (s + 1) % sections * count + (i ^ GROUP))
        for s in range(sections)
        for i in range(count)
    ]
    return lax.ppermute(value, ("section", "expert"), route)


def head(value):
    return lax.reduce_precision(value, exponent_bits=8, mantissa_bits=7)


def in_three(value):
    first = head(value)
    second = head(value - first)
    third = head(value - first - second)
    return [part.astype(jnp.bfloat16) for part in (first, second, third)]


def take(value, index, axis):
    return lax.dynamic_index_in_dim(value, index, axis, keepdims=False)


def from_sibling(quarters, core):
    near = swap(take(quarters, 1 - core, 1), 1)
    return jnp.stack([take(quarters, core, 1), near], axis=1)


def from_chip(both, chip):
    return take(both, chip, 0), swap(take(both, 1 - chip, 0), 2)


def tables(ids, gates, half, peers, rows_dev):
    rows = ids.shape[0]
    wanted = 2 * jnp.arange(peers, dtype=jnp.int32) + half
    hit = ids.T[None, :, :] == wanted[:, None, None]
    routed = jnp.any(hit, axis=1)
    weight = jnp.sum(jnp.where(hit, gates.T[None, :, :], 0.0), axis=1)
    at = jnp.arange(rows, dtype=jnp.int32)
    before = (at[:, None] < at[None, :]) & (at[:, None] // rows_dev == at[None, :] // rows_dev)
    rank = jnp.dot(
        routed.astype(jnp.bfloat16), before.astype(jnp.bfloat16), preferred_element_type=jnp.float32
    ).astype(jnp.int32)
    slots = rows // rows_dev * CAP
    slot = jnp.arange(slots, dtype=jnp.int32)
    mine = (slot[:, None] // CAP == at[None, :] // rows_dev)[None]
    picked = mine & routed[:, None, :] & (rank[:, None, :] == (slot % CAP)[None, :, None])
    weigher = jnp.where(picked, weight[:, None, :], 0.0)
    shape = (peers * slots, rows)
    return picked.astype(jnp.bfloat16).reshape(shape), weigher.reshape(shape)


def normed_quarters(current, gain):
    values = current.astype(jnp.float32)
    inverse_rms = lax.rsqrt(jnp.mean(values * values, axis=-1, keepdims=True) + 1e-06)
    normed = (values * inverse_rms * gain).astype(jnp.bfloat16)
    return normed.reshape(current.shape[0], PAIR, -1).transpose(1, 0, 2)


def body(hidden, norm_gain, w_up, w_down, expert_ids, route_gates):
    width = hidden.shape[-1]
    rows_dev = hidden.shape[1]
    passes, top = expert_ids.shape[1], expert_ids.shape[-1]
    count = lax.axis_size("expert")
    peers = count // (GROUP * HALVES)
    part = width // PAIR
    block = GROUP * rows_dev
    total = HALVES * block
    same_row, same_place = groups(count)
    place = lax.axis_index("expert")
    core, chip, half = place % 2, place // 2 % 2, place // GROUP % HALVES
    if passes % 2:
        raise ValueError("odd passes")
    gain = norm_gain[0]
    current = hidden[0]

    facts = [expert_ids[0].astype(jnp.bfloat16)] + in_three(route_gates[0])
    facts = jnp.stack(facts).transpose(2, 0, 1, 3).reshape(rows_dev, -1)
    facts = jnp.pad(facts, ((0, 0), (0, LANES - facts.shape[1])))

    for t in range(passes):
        sent = normed_quarters(current, gain)
        if t == 0:
            facts = jnp.broadcast_to(facts[None], (PAIR, rows_dev, LANES))
            sent = jnp.concatenate([sent, facts], axis=2)
        sent = jnp.concatenate([sent] * (2 * HALVES))
        arrived = exchange(sent, same_row)
        if t == 0:
            up_both = from_sibling(w_up[0].reshape(2, 2, part, HID_DEV), core)
            w_down, up_both = lax.optimization_barrier((w_down, up_both))
            up, up_far = from_chip(up_both, chip)
            down = w_down[0].reshape(HID_DEV, 2, 2, part).transpose(1, 2, 0, 3)
            down, down_far = from_chip(from_sibling(down, core), chip)
            arrived, up, up_far, down = lax.optimization_barrier((arrived, up, up_far, down))
            up = [up[0], up[1], up_far[0], up_far[1]]
            facts = arrived[:, :, part:].astype(jnp.float32).reshape(total, LANES)
            routes = facts[:, : 4 * passes * top].reshape(total, 4, passes, top)
            arrived = arrived[:, :, :part]
        arrived = arrived.reshape(HALVES, block, part)
        if t % 2 == 1:
            arrived = jnp.concatenate([arrived[1:], arrived[:1]])
        rows = arrived.reshape(total, part)

        ids = routes[:, 0, t].astype(jnp.int32)
        gates = jnp.sum(routes[:, 1:, t], axis=1)
        picker, weigher = tables(ids, gates, half, peers, rows_dev)
        slots = jnp.dot(picker, rows, preferred_element_type=jnp.float32).astype(jnp.bfloat16)
        slots = exchange(slots, same_place)
        if t == 0:
            slots, down_far = lax.optimization_barrier((slots, down_far))
            down = jnp.concatenate([down, down_far]).reshape(PAIR * HID_DEV, part)
        sums = [jnp.dot(slots, up[k], preferred_element_type=jnp.float32) for k in range(PAIR)]
        came = swap(jnp.stack([sums[1], sums[3]]), 1)
        came_far = swap(sums[2] + came[1], 2)
        active = jax.nn.silu(sums[0] + came[0] + came_far).astype(jnp.bfloat16)
        active = jnp.stack([active, swap(active, 1)])
        active = jnp.concatenate([active, swap(active, 2)])
        active = jnp.concatenate([active[k] for k in range(PAIR)], axis=1)
        outputs = jnp.dot(active, down, preferred_element_type=jnp.float32).astype(jnp.bfloat16)
        outputs = exchange(outputs, same_place)
        mixture = jnp.dot(
            weigher.T,
            outputs.astype(jnp.float32),
            precision=lax.Precision.HIGHEST,
            preferred_element_type=jnp.float32,
        )
        mixture = mixture.astype(jnp.bfloat16).reshape(HALVES, GROUP, rows_dev, part)
        if t % 2 == 1:
            mixture = jnp.concatenate([mixture[1:], mixture[:1]])
        came = exchange(mixture.reshape(HALVES * GROUP, rows_dev, part), same_row)
        came = came.reshape(2 * HALVES, PAIR, rows_dev, part)
        came = jnp.sum(came.astype(jnp.float32), axis=0).transpose(1, 0, 2)
        updated = current.astype(jnp.float32) + came.reshape(rows_dev, width)
        current = next_section(updated.astype(jnp.bfloat16))
    return current[None]


def solution(mesh):
    placed = (
        P("section", "expert", None),
        P("section", None),
        P("section", None, "expert"),
        P("section", "expert", None),
        P("section", None, "expert", None),
        P("section", None, "expert", None),
    )
    return jax.shard_map(
        body, mesh=mesh, in_specs=placed, out_specs=P("section", "expert", None), check_vma=False
    )
```

```python
import jax
import jax.numpy as jnp
from jax import lax
from jax.sharding import PartitionSpec as P

HID = 1024
HID_DEV = 128
GROUP = HID // HID_DEV
PAIR = 4
CAP = 4
HALVES = 2
LANES = 128


def groups(count):
    span = GROUP * HALVES
    same_row = [[first + k for k in range(span)] for first in range(0, count, span)]
    same_place = [[first + k for first in range(0, count, span)] for k in range(span)]
    return same_row, same_place


def exchange(value, within):
    return lax.all_to_all(
        value, "expert", split_axis=0, concat_axis=0, axis_index_groups=within, tiled=True
    )


def swap(value, bit):
    count = lax.axis_size("expert")
    return lax.ppermute(value, "expert", [(i, i ^ bit) for i in range(count)])


def next_section(value):
    sections, count = lax.axis_size("section"), lax.axis_size("expert")
    route = [
        (s * count + i, (s + 1) % sections * count + (i ^ GROUP))
        for s in range(sections)
        for i in range(count)
    ]
    return lax.ppermute(value, ("section", "expert"), route)


def head(value):
    return lax.reduce_precision(value, exponent_bits=8, mantissa_bits=7)


def in_three(value):
    first = head(value)
    second = head(value - first)
    third = head(value - first - second)
    return [part.astype(jnp.bfloat16) for part in (first, second, third)]


def take(value, index, axis):
    return lax.dynamic_index_in_dim(value, index, axis, keepdims=False)


def from_sibling(keep, give):
    return jnp.stack([keep, swap(give, 1)], axis=1)


def for_chip(both, chip):
    return take(both, chip, 0), take(both, 1 - chip, 0)


def tables(ids, gates, half, peers, rows_dev):
    rows = ids.shape[0]
    wanted = 2 * jnp.arange(peers, dtype=jnp.int32) + half
    hit = ids.T[None, :, :] == wanted[:, None, None]
    routed = jnp.any(hit, axis=1)
    weight = jnp.sum(jnp.where(hit, gates.T[None, :, :], 0.0), axis=1)
    at = jnp.arange(rows, dtype=jnp.int32)
    before = (at[:, None] < at[None, :]) & (at[:, None] // rows_dev == at[None, :] // rows_dev)
    rank = jnp.dot(
        routed.astype(jnp.bfloat16), before.astype(jnp.bfloat16), preferred_element_type=jnp.float32
    ).astype(jnp.int32)
    slots = rows // rows_dev * CAP
    slot = jnp.arange(slots, dtype=jnp.int32)
    mine = (slot[:, None] // CAP == at[None, :] // rows_dev)[None]
    picked = mine & routed[:, None, :] & (rank[:, None, :] == (slot % CAP)[None, :, None])
    weigher = jnp.where(picked, weight[:, None, :], 0.0)
    shape = (peers * slots, rows)
    return picked.astype(jnp.bfloat16).reshape(shape), weigher.reshape(shape)


def normed_quarters(current, gain):
    values = current.astype(jnp.float32)
    inverse_rms = lax.rsqrt(jnp.mean(values * values, axis=-1, keepdims=True) + 1e-06)
    normed = (values * inverse_rms * gain).astype(jnp.bfloat16)
    return normed.reshape(current.shape[0], PAIR, -1).transpose(1, 0, 2)


def body(hidden, norm_gain, w_up, w_down, expert_ids, route_gates):
    width = hidden.shape[-1]
    rows_dev = hidden.shape[1]
    passes, top = expert_ids.shape[1], expert_ids.shape[-1]
    count = lax.axis_size("expert")
    peers = count // (GROUP * HALVES)
    part = width // PAIR
    block = GROUP * rows_dev
    total = HALVES * block
    same_row, same_place = groups(count)
    place = lax.axis_index("expert")
    core, chip, half = place % 2, place // 2 % 2, place // GROUP % HALVES
    if passes % 2:
        raise ValueError("odd passes")
    gain = norm_gain[0]
    current = hidden[0]

    facts = [expert_ids[0].astype(jnp.bfloat16)] + in_three(route_gates[0])
    facts = jnp.stack(facts).transpose(2, 0, 1, 3).reshape(rows_dev, -1)
    facts = jnp.pad(facts, ((0, 0), (0, LANES - facts.shape[1])))

    for t in range(passes):
        sent = normed_quarters(current, gain)
        if t == 0:
            facts = jnp.broadcast_to(facts[None], (PAIR, rows_dev, LANES))
            sent = jnp.concatenate([sent, facts], axis=2)
        sent = jnp.concatenate([sent] * (2 * HALVES))
        arrived = exchange(sent, same_row)
        if t == 0:
            quarters = w_up[0].reshape(2, 2, part, HID_DEV)
            up_both = from_sibling(take(quarters, core, 1), take(quarters, 1 - core, 1))
            up, give = for_chip(up_both, chip)
            core, give = lax.optimization_barrier((core, give))
            up_far = swap(give, 2)
            quarters = [w_down[0, :, k * part : (k + 1) * part] for k in range(PAIR)]
            even, odd = jnp.stack(quarters[0::2]), jnp.stack(quarters[1::2])
            keep, give = jnp.where(core == 0, even, odd), jnp.where(core == 0, odd, even)
            down, give = for_chip(from_sibling(keep, give), chip)
            down_far = swap(give, 2)
            arrived, up, up_far, down = lax.optimization_barrier((arrived, up, up_far, down))
            up = [up[0], up[1], up_far[0], up_far[1]]
            facts = arrived[:, :, part:].astype(jnp.float32).reshape(total, LANES)
            routes = facts[:, : 4 * passes * top].reshape(total, 4, passes, top)
            arrived = arrived[:, :, :part]
        arrived = arrived.reshape(HALVES, block, part)
        if t % 2 == 1:
            arrived = jnp.concatenate([arrived[1:], arrived[:1]])
        rows = arrived.reshape(total, part)

        ids = routes[:, 0, t].astype(jnp.int32)
        gates = jnp.sum(routes[:, 1:, t], axis=1)
        picker, weigher = tables(ids, gates, half, peers, rows_dev)
        slots = jnp.dot(picker, rows, preferred_element_type=jnp.float32).astype(jnp.bfloat16)
        slots = exchange(slots, same_place)
        if t == 0:
            slots, down_far = lax.optimization_barrier((slots, down_far))
            down = jnp.concatenate([down, down_far]).reshape(PAIR * HID_DEV, part)
        sums = [jnp.dot(slots, up[k], preferred_element_type=jnp.float32) for k in range(PAIR)]
        came = swap(jnp.stack([sums[1], sums[3]]), 1)
        came_far = swap(sums[2] + came[1], 2)
        active = jax.nn.silu(sums[0] + came[0] + came_far).astype(jnp.bfloat16)
        active = jnp.stack([active, swap(active, 1)])
        active = jnp.concatenate([active, swap(active, 2)])
        active = jnp.concatenate([active[k] for k in range(PAIR)], axis=1)
        outputs = jnp.dot(active, down, preferred_element_type=jnp.float32).astype(jnp.bfloat16)
        outputs = exchange(outputs, same_place)
        mixture = jnp.dot(
            weigher.T,
            outputs.astype(jnp.float32),
            precision=lax.Precision.HIGHEST,
            preferred_element_type=jnp.float32,
        )
        mixture = mixture.astype(jnp.bfloat16).reshape(HALVES, GROUP, rows_dev, part)
        if t % 2 == 1:
            mixture = jnp.concatenate([mixture[1:], mixture[:1]])
        came = exchange(mixture.reshape(HALVES * GROUP, rows_dev, part), same_row)
        came = came.reshape(2 * HALVES, PAIR, rows_dev, part)
        came = jnp.sum(came.astype(jnp.float32), axis=0).transpose(1, 0, 2)
        updated = current.astype(jnp.float32) + came.reshape(rows_dev, width)
        current = next_section(updated.astype(jnp.bfloat16))
    return current[None]


def solution(mesh):
    placed = (
        P("section", "expert", None),
        P("section", None),
        P("section", None, "expert"),
        P("section", "expert", None),
        P("section", None, "expert", None),
        P("section", None, "expert", None),
    )
    return jax.shard_map(
        body, mesh=mesh, in_specs=placed, out_specs=P("section", "expert", None), check_vma=False
    )
```

```python
import jax
import jax.numpy as jnp
from jax import lax
from jax.sharding import PartitionSpec as P

HID = 1024
HID_DEV = 128
GROUP = HID // HID_DEV
PAIR = 4
CAP = 4
HALVES = 2
LANES = 128


def groups(count):
    span = GROUP * HALVES
    same_row = [[first + k for k in range(span)] for first in range(0, count, span)]
    same_place = [[first + k for first in range(0, count, span)] for k in range(span)]
    return same_row, same_place


def exchange(value, within):
    return lax.all_to_all(
        value, "expert", split_axis=0, concat_axis=0, axis_index_groups=within, tiled=True
    )


def swap(value, bit):
    count = lax.axis_size("expert")
    return lax.ppermute(value, "expert", [(i, i ^ bit) for i in range(count)])


def next_section(value):
    sections, count = lax.axis_size("section"), lax.axis_size("expert")
    route = [
        (s * count + i, (s + 1) % sections * count + (i ^ GROUP))
        for s in range(sections)
        for i in range(count)
    ]
    return lax.ppermute(value, ("section", "expert"), route)


def head(value):
    return lax.reduce_precision(value, exponent_bits=8, mantissa_bits=7)


def in_three(value):
    first = head(value)
    second = head(value - first)
    third = head(value - first - second)
    return [part.astype(jnp.bfloat16) for part in (first, second, third)]


def take(value, index, axis):
    return lax.dynamic_index_in_dim(value, index, axis, keepdims=False)


def from_sibling(keep, give):
    return jnp.stack([keep, swap(give, 1)], axis=1)


def for_chip(both, chip):
    return take(both, chip, 0), take(both, 1 - chip, 0)


def tables(ids, gates, half, peers, rows_dev):
    rows = ids.shape[0]
    wanted = 2 * jnp.arange(peers, dtype=jnp.int32) + half
    hit = ids.T[None, :, :] == wanted[:, None, None]
    routed = jnp.any(hit, axis=1)
    weight = jnp.sum(jnp.where(hit, gates.T[None, :, :], 0.0), axis=1)
    at = jnp.arange(rows, dtype=jnp.int32)
    before = (at[:, None] < at[None, :]) & (at[:, None] // rows_dev == at[None, :] // rows_dev)
    rank = jnp.dot(
        routed.astype(jnp.bfloat16), before.astype(jnp.bfloat16), preferred_element_type=jnp.float32
    ).astype(jnp.int32)
    slots = rows // rows_dev * CAP
    slot = jnp.arange(slots, dtype=jnp.int32)
    mine = (slot[:, None] // CAP == at[None, :] // rows_dev)[None]
    picked = mine & routed[:, None, :] & (rank[:, None, :] == (slot % CAP)[None, :, None])
    weigher = jnp.where(picked, weight[:, None, :], 0.0)
    shape = (peers * slots, rows)
    return picked.astype(jnp.bfloat16).reshape(shape), weigher.reshape(shape)


def normed_quarters(current, gain):
    values = current.astype(jnp.float32)
    inverse_rms = lax.rsqrt(jnp.mean(values * values, axis=-1, keepdims=True) + 1e-06)
    normed = (values * inverse_rms * gain).astype(jnp.bfloat16)
    return normed.reshape(current.shape[0], PAIR, -1).transpose(1, 0, 2)


def body(hidden, norm_gain, w_up, w_down, expert_ids, route_gates):
    width = hidden.shape[-1]
    rows_dev = hidden.shape[1]
    passes, top = expert_ids.shape[1], expert_ids.shape[-1]
    count = lax.axis_size("expert")
    peers = count // (GROUP * HALVES)
    part = width // PAIR
    block = GROUP * rows_dev
    total = HALVES * block
    same_row, same_place = groups(count)
    place = lax.axis_index("expert")
    core, chip, half = place % 2, place // 2 % 2, place // GROUP % HALVES
    if passes % 2:
        raise ValueError("odd passes")
    gain = norm_gain[0]
    current = hidden[0]

    facts = [expert_ids[0].astype(jnp.bfloat16)] + in_three(route_gates[0])
    facts = jnp.stack(facts).transpose(2, 0, 1, 3).reshape(rows_dev, -1)
    facts = jnp.pad(facts, ((0, 0), (0, LANES - facts.shape[1])))

    for t in range(passes):
        sent = normed_quarters(current, gain)
        if t == 0:
            facts = jnp.broadcast_to(facts[None], (PAIR, rows_dev, LANES))
            sent = jnp.concatenate([sent, facts], axis=2)
        sent = jnp.concatenate([sent] * (2 * HALVES))
        arrived = exchange(sent, same_row)
        if t == 0:
            quarters = w_up[0].reshape(2, 2, part, HID_DEV)
            up_both = from_sibling(take(quarters, core, 1), take(quarters, 1 - core, 1))
            up, give = for_chip(up_both, chip)
            core, give = lax.optimization_barrier((core, give))
            up_far = swap(give, 2)
            quarters = [w_down[0, :, k * part : (k + 1) * part] for k in range(PAIR)]
            even, odd = jnp.stack(quarters[0::2]), jnp.stack(quarters[1::2])
            keep, give = jnp.where(core == 0, even, odd), jnp.where(core == 0, odd, even)
            down, give = for_chip(from_sibling(keep, give), chip)
            arrived, up, up_far, give = lax.optimization_barrier((arrived, up, up_far, give))
            down_far = swap(give, 2)
            up = [up[0], up[1], up_far[0], up_far[1]]
            facts = arrived[:, :, part:].astype(jnp.float32).reshape(total, LANES)
            routes = facts[:, : 4 * passes * top].reshape(total, 4, passes, top)
            arrived = arrived[:, :, :part]
        arrived = arrived.reshape(HALVES, block, part)
        if t % 2 == 1:
            arrived = jnp.concatenate([arrived[1:], arrived[:1]])
        rows = arrived.reshape(total, part)

        ids = routes[:, 0, t].astype(jnp.int32)
        gates = jnp.sum(routes[:, 1:, t], axis=1)
        picker, weigher = tables(ids, gates, half, peers, rows_dev)
        slots = jnp.dot(picker, rows, preferred_element_type=jnp.float32).astype(jnp.bfloat16)
        slots = exchange(slots, same_place)
        sums = [jnp.dot(slots, up[k], preferred_element_type=jnp.float32) for k in range(PAIR)]
        came = swap(jnp.stack([sums[1], sums[3]]), 1)
        if t == 0:
            came, down_far = lax.optimization_barrier((came, down_far))
            down = jnp.concatenate([down, down_far]).reshape(PAIR * HID_DEV, part)
        came_far = swap(sums[2] + came[1], 2)
        active = jax.nn.silu(sums[0] + came[0] + came_far).astype(jnp.bfloat16)
        active = jnp.stack([active, swap(active, 1)])
        active = jnp.concatenate([active, swap(active, 2)])
        active = jnp.concatenate([active[k] for k in range(PAIR)], axis=1)
        outputs = jnp.dot(active, down, preferred_element_type=jnp.float32).astype(jnp.bfloat16)
        outputs = exchange(outputs, same_place)
        mixture = jnp.dot(
            weigher.T,
            outputs.astype(jnp.float32),
            precision=lax.Precision.HIGHEST,
            preferred_element_type=jnp.float32,
        )
        mixture = mixture.astype(jnp.bfloat16).reshape(HALVES, GROUP, rows_dev, part)
        if t % 2 == 1:
            mixture = jnp.concatenate([mixture[1:], mixture[:1]])
        came = exchange(mixture.reshape(HALVES * GROUP, rows_dev, part), same_row)
        came = came.reshape(2 * HALVES, PAIR, rows_dev, part)
        came = jnp.sum(came.astype(jnp.float32), axis=0).transpose(1, 0, 2)
        updated = current.astype(jnp.float32) + came.reshape(rows_dev, width)
        current = next_section(updated.astype(jnp.bfloat16))
    return current[None]


def solution(mesh):
    placed = (
        P("section", "expert", None),
        P("section", None),
        P("section", None, "expert"),
        P("section", "expert", None),
        P("section", None, "expert", None),
        P("section", None, "expert", None),
    )
    return jax.shard_map(
        body, mesh=mesh, in_specs=placed, out_specs=P("section", "expert", None), check_vma=False
    )
```

```python
import jax
import jax.numpy as jnp
from jax import lax
from jax.sharding import PartitionSpec as P

HID = 1024
HID_DEV = 128
GROUP = HID // HID_DEV
PAIR = 4
CAP = 4
HALVES = 2
LANES = 128


def groups(count):
    span = GROUP * HALVES
    same_row = [[first + k for k in range(span)] for first in range(0, count, span)]
    same_place = [[first + k for first in range(0, count, span)] for k in range(span)]
    return same_row, same_place


def exchange(value, within):
    return lax.all_to_all(
        value, "expert", split_axis=0, concat_axis=0, axis_index_groups=within, tiled=True
    )


def swap(value, bit):
    count = lax.axis_size("expert")
    return lax.ppermute(value, "expert", [(i, i ^ bit) for i in range(count)])


def next_section(value):
    sections, count = lax.axis_size("section"), lax.axis_size("expert")
    route = [
        (s * count + i, (s + 1) % sections * count + (i ^ GROUP))
        for s in range(sections)
        for i in range(count)
    ]
    return lax.ppermute(value, ("section", "expert"), route)


def head(value):
    return lax.reduce_precision(value, exponent_bits=8, mantissa_bits=7)


def in_three(value):
    first = head(value)
    second = head(value - first)
    third = head(value - first - second)
    return [part.astype(jnp.bfloat16) for part in (first, second, third)]


def take(value, index, axis):
    return lax.dynamic_index_in_dim(value, index, axis, keepdims=False)


def from_sibling(keep, give):
    return jnp.stack([keep, swap(give, 1)], axis=1)


def for_chip(both, chip):
    return take(both, chip, 0), take(both, 1 - chip, 0)


def tables(ids, gates, half, peers, rows_dev):
    rows = ids.shape[0]
    wanted = 2 * jnp.arange(peers, dtype=jnp.int32) + half
    hit = ids.T[None, :, :] == wanted[:, None, None]
    routed = jnp.any(hit, axis=1)
    weight = jnp.sum(jnp.where(hit, gates.T[None, :, :], 0.0), axis=1)
    at = jnp.arange(rows, dtype=jnp.int32)
    before = (at[:, None] < at[None, :]) & (at[:, None] // rows_dev == at[None, :] // rows_dev)
    rank = jnp.dot(
        routed.astype(jnp.bfloat16), before.astype(jnp.bfloat16), preferred_element_type=jnp.float32
    ).astype(jnp.int32)
    slots = rows // rows_dev * CAP
    slot = jnp.arange(slots, dtype=jnp.int32)
    mine = (slot[:, None] // CAP == at[None, :] // rows_dev)[None]
    picked = mine & routed[:, None, :] & (rank[:, None, :] == (slot % CAP)[None, :, None])
    weigher = jnp.where(picked, weight[:, None, :], 0.0)
    shape = (peers * slots, rows)
    return picked.astype(jnp.bfloat16).reshape(shape), weigher.reshape(shape)


def normed_quarters(current, gain):
    values = current.astype(jnp.float32)
    inverse_rms = lax.rsqrt(jnp.mean(values * values, axis=-1, keepdims=True) + 1e-06)
    normed = (values * inverse_rms * gain).astype(jnp.bfloat16)
    return normed.reshape(current.shape[0], PAIR, -1).transpose(1, 0, 2)


def body(hidden, norm_gain, w_up, w_down, expert_ids, route_gates):
    width = hidden.shape[-1]
    rows_dev = hidden.shape[1]
    passes, top = expert_ids.shape[1], expert_ids.shape[-1]
    count = lax.axis_size("expert")
    peers = count // (GROUP * HALVES)
    part = width // PAIR
    block = GROUP * rows_dev
    total = HALVES * block
    same_row, same_place = groups(count)
    place = lax.axis_index("expert")
    core, chip, half = place % 2, place // 2 % 2, place // GROUP % HALVES
    if passes % 2:
        raise ValueError("odd passes")
    gain = norm_gain[0]
    current = hidden[0]

    facts = [expert_ids[0].astype(jnp.bfloat16)] + in_three(route_gates[0])
    facts = jnp.stack(facts).transpose(2, 0, 1, 3).reshape(rows_dev, -1)
    facts = jnp.pad(facts, ((0, 0), (0, LANES - facts.shape[1])))

    for t in range(passes):
        sent = normed_quarters(current, gain)
        if t == 0:
            facts = jnp.broadcast_to(facts[None], (PAIR, rows_dev, LANES))
            sent = jnp.concatenate([sent, facts], axis=2)
        sent = jnp.concatenate([sent] * (2 * HALVES))
        arrived = exchange(sent, same_row)
        if t == 0:
            quarters = w_up[0].reshape(2, 2, part, HID_DEV)
            up_both = from_sibling(take(quarters, core, 1), take(quarters, 1 - core, 1))
            up, give = for_chip(up_both, chip)
            core, give = lax.optimization_barrier((core, give))
            up_far = swap(give, 2)
            quarters = [w_down[0, :, k * part : (k + 1) * part] for k in range(PAIR)]
            even, odd = jnp.stack(quarters[0::2]), jnp.stack(quarters[1::2])
            keep, give = jnp.where(core == 0, even, odd), jnp.where(core == 0, odd, even)
            down, give = for_chip(from_sibling(keep, give), chip)
            down_far = swap(give, 2)
            arrived, up, down = lax.optimization_barrier((arrived, up, down))
            facts = arrived[:, :, part:].astype(jnp.float32).reshape(total, LANES)
            routes = facts[:, : 4 * passes * top].reshape(total, 4, passes, top)
            arrived = arrived[:, :, :part]
        arrived = arrived.reshape(HALVES, block, part)
        if t % 2 == 1:
            arrived = jnp.concatenate([arrived[1:], arrived[:1]])
        rows = arrived.reshape(total, part)

        ids = routes[:, 0, t].astype(jnp.int32)
        gates = jnp.sum(routes[:, 1:, t], axis=1)
        picker, weigher = tables(ids, gates, half, peers, rows_dev)
        slots = jnp.dot(picker, rows, preferred_element_type=jnp.float32).astype(jnp.bfloat16)
        slots = exchange(slots, same_place)
        if t == 0:
            slots, up_far, down_far = lax.optimization_barrier((slots, up_far, down_far))
            up = [up[0], up[1], up_far[0], up_far[1]]
            down = jnp.concatenate([down, down_far]).reshape(PAIR * HID_DEV, part)
        sums = [jnp.dot(slots, up[k], preferred_element_type=jnp.float32) for k in range(PAIR)]
        came = swap(jnp.stack([sums[1], sums[3]]), 1)
        came_far = swap(sums[2] + came[1], 2)
        active = jax.nn.silu(sums[0] + came[0] + came_far).astype(jnp.bfloat16)
        active = jnp.stack([active, swap(active, 1)])
        active = jnp.concatenate([active, swap(active, 2)])
        active = jnp.concatenate([active[k] for k in range(PAIR)], axis=1)
        outputs = jnp.dot(active, down, preferred_element_type=jnp.float32).astype(jnp.bfloat16)
        outputs = exchange(outputs, same_place)
        mixture = jnp.dot(
            weigher.T,
            outputs.astype(jnp.float32),
            precision=lax.Precision.HIGHEST,
            preferred_element_type=jnp.float32,
        )
        mixture = mixture.astype(jnp.bfloat16).reshape(HALVES, GROUP, rows_dev, part)
        if t % 2 == 1:
            mixture = jnp.concatenate([mixture[1:], mixture[:1]])
        came = exchange(mixture.reshape(HALVES * GROUP, rows_dev, part), same_row)
        came = came.reshape(2 * HALVES, PAIR, rows_dev, part)
        came = jnp.sum(came.astype(jnp.float32), axis=0).transpose(1, 0, 2)
        updated = current.astype(jnp.float32) + came.reshape(rows_dev, width)
        current = next_section(updated.astype(jnp.bfloat16))
    return current[None]


def solution(mesh):
    placed = (
        P("section", "expert", None),
        P("section", None),
        P("section", None, "expert"),
        P("section", "expert", None),
        P("section", None, "expert", None),
        P("section", None, "expert", None),
    )
    return jax.shard_map(
        body, mesh=mesh, in_specs=placed, out_specs=P("section", "expert", None), check_vma=False
    )
```
